256 devices in a mesh: row: 16 (over z, x_lo), col: 16 (over y, x_hi, core).
Axes of the slice: x: 4 (x_hi: 2, x_lo: 2; x = x_hi * 2 + x_lo), y: 4, z: 8, core: 2. Of those that a mesh axis runs over, the one named last changes fastest.
Arguments:
- pair: bfloat16 [512, 512, 128], P('row', 'col'), may hold values from -6 to 6
- pair_mask: int32 [512, 512], P('row', 'col'), may hold values from 0 to 1, as said below
- proj_weight: bfloat16 [128, 640], replicated, may hold values from -0.5 to 0.5
- out_weight: bfloat16 [128, 128], replicated, may hold values from -0.5 to 0.5
- in_gain: float32 [128], replicated, may hold values from 0.5 to 1.5
- out_gain: float32 [128], replicated, may hold values from 0.5 to 1.5
- cotangent: bfloat16 [512, 512, 128], P('row', 'col'), may hold values from -6 to 6
Outputs:
- d_pair: float32 [512, 512, 128], P('row', 'col')
- d_proj_weight: float32 [128, 640], replicated
- d_out_weight: float32 [128, 128], replicated
- d_in_gain: float32 [128], replicated
- d_out_gain: float32 [128], replicated
The draws below stay inside these ranges and needn't reach their ends.
Inputs may be any that keep to these rules, and one draw needn't show every extreme that they name: pair_mask[i, j] is the product of a 0/1 flag of token i and the same flag of token j.
All inputs are finite; a program needn't handle non-finite values.
Results may differ from the reference program's by a relative error of at most 0.019.
Values may be sent and summed in bfloat16 or wider, within the bound.
A program may use at most 128 MiB of HBM per device.

```python
import jax
import jax.numpy as jnp
from jax import lax

C = 128
N = 512


def draw_pair_mask(key, part):
    flags = jax.random.randint(key, (N,), 0, 6)
    valid = (flags != 0).astype(jnp.int32)
    return valid[:, None] * valid[None, :]


def level_of(rng, dims, split, least, top_value):
    def one(position, shards_of):
        steps = jax.random.uniform(jax.random.fold_in(jax.random.fold_in(rng, 6), position), (shards_of,), jnp.float32, least / len(split), top_value / len(split))
        return jnp.repeat(jnp.exp(steps), dims[position] // shards_of).reshape((-1,) + (1,) * (len(dims) - position - 1))

    level = one(*split[0])
    for cut in split[1:]:
        level = level * one(*cut)
    return level


def normal_values(stream_key, extent, scale, bound, shards=(), kind=jnp.bfloat16):
    level = level_of(stream_key, extent, shards, -0.22, 0.18) if shards else 1.0
    array = jax.random.normal(stream_key, extent, jnp.float32) * scale * level
    return jnp.minimum(jnp.maximum(array, -bound), bound).astype(kind)


def setup_inputs(seed: int = 0) -> dict:
    seeds = jax.random.split(jax.random.key(seed), 8)
    return {
        "pair": normal_values(seeds[0], (N, N, C), 1.0, 6.0, ((0, 16), (1, 16))),
        "pair_mask": draw_pair_mask(jax.random.fold_in(seeds[7], 71), 0),
        "proj_weight": normal_values(seeds[2], (C, 5 * C), C ** -0.5, 0.5),
        "out_weight": normal_values(seeds[3], (C, C), C ** -0.5, 0.5),
        "in_gain": jnp.clip(jax.random.uniform(seeds[4], (C,), jnp.float32, 0.5, 1.5), 0.5, 1.5),
        "out_gain": jnp.clip(jax.random.uniform(seeds[5], (C,), jnp.float32, 0.5, 1.5), 0.5, 1.5),
        "cotangent": normal_values(seeds[6], (N, N, C), 1.0, 6.0, ((0, 16), (1, 16))),
    }


def normalize(values):
    average = lax.optimization_barrier(jnp.mean(values, axis=-1, keepdims=True))
    centred = values - average
    spread = lax.optimization_barrier(jnp.mean(centred * centred, axis=-1, keepdims=True))
    inverse = lax.rsqrt(spread + 1e-05)
    return (centred * inverse, inverse)

def layer_back(grad_hat, normed, inverse):
    first_mean = lax.optimization_barrier(jnp.mean(grad_hat, axis=-1, keepdims=True))
    second_mean = lax.optimization_barrier(jnp.mean(grad_hat * normed, axis=-1, keepdims=True))
    return (grad_hat - first_mean - normed * second_mean) * inverse

def reference(pair, pair_mask, proj_weight, out_weight, in_gain, out_gain, cotangent):
    channels = pair.shape[2]
    total = pair.shape[0]
    normed, inverse = normalize(pair.astype(jnp.float32))
    zn = (normed * in_gain).astype(jnp.bfloat16)
    flat_zn = zn.reshape(-1, channels)
    linear = jnp.dot(flat_zn, proj_weight, preferred_element_type=jnp.float32).reshape(total, total, 5 * channels)
    proj_left = linear[..., 0:channels]
    gate_left = linear[..., channels:2 * channels]
    proj_right = linear[..., 2 * channels:3 * channels]
    gate_right = linear[..., 3 * channels:4 * channels]
    gate_out = linear[..., 4 * channels:]
    mask_f = pair_mask.astype(jnp.float32)[..., None]
    sig_left = jax.nn.sigmoid(gate_left)
    sig_right = jax.nn.sigmoid(gate_right)
    left = (mask_f * sig_left * proj_left).astype(jnp.bfloat16)
    right = (mask_f * sig_right * proj_right).astype(jnp.bfloat16)
    left_f = left.astype(jnp.float32)
    right_f = right.astype(jnp.float32)
    triangle = jnp.einsum('kic,kjc->ijc', left_f, right_f)
    tri_hat, tri_inv = normalize(triangle)
    onorm = (tri_hat * out_gain).astype(jnp.bfloat16)
    flat_on = onorm.reshape(-1, channels)
    projected = jnp.dot(flat_on, out_weight, preferred_element_type=jnp.float32).reshape(total, total, channels)
    sig_gate = jax.nn.sigmoid(gate_out)
    cot_f = cotangent.astype(jnp.float32)
    dproj = (cot_f * sig_gate).astype(jnp.bfloat16)
    dgate = cot_f * projected * sig_gate * (1.0 - sig_gate)
    flat_dproj = dproj.reshape(-1, channels)
    d_out_weight = jnp.dot(flat_on.T, flat_dproj, preferred_element_type=jnp.float32) / total
    donorm = jnp.dot(flat_dproj, out_weight.T, preferred_element_type=jnp.float32).reshape(total, total, channels)
    d_out_gain = lax.optimization_barrier(jnp.sum(donorm * tri_hat, axis=(0, 1))) / total
    dtri = layer_back(donorm * out_gain, tri_hat, tri_inv).astype(jnp.bfloat16)
    dtri_f = dtri.astype(jnp.float32)
    dleft = jnp.einsum('kjc,ijc->kic', right_f, dtri_f)
    dright = jnp.einsum('kic,ijc->kjc', left_f, dtri_f)
    dlin = jnp.concatenate([dleft * mask_f * sig_left, dleft * mask_f * proj_left * sig_left * (1.0 - sig_left), dright * mask_f * sig_right, dright * mask_f * proj_right * sig_right * (1.0 - sig_right), dgate], axis=-1).astype(jnp.bfloat16)
    flat_dlin = dlin.reshape(-1, 5 * channels)
    d_proj_weight = jnp.dot(flat_zn.T, flat_dlin, preferred_element_type=jnp.float32) / total
    dzn = jnp.dot(flat_dlin, proj_weight.T, preferred_element_type=jnp.float32).reshape(total, total, channels)
    d_in_gain = lax.optimization_barrier(jnp.sum(dzn * normed, axis=(0, 1))) / total
    d_pair = layer_back(dzn * in_gain, normed, inverse)
    return (d_pair, d_proj_weight, d_out_weight, d_in_gain, d_out_gain)
```

```python
import jax
import jax.numpy as jnp
from jax import lax
from jax.sharding import PartitionSpec as P


def normalize(values):
    average = jnp.mean(values, axis=-1, keepdims=True)
    centred = values - average
    spread = jnp.mean(centred * centred, axis=-1, keepdims=True)
    inverse = lax.rsqrt(spread + 1e-05)
    return (centred * inverse, inverse)


def layer_back(grad_hat, normed, inverse):
    first_mean = jnp.mean(grad_hat, axis=-1, keepdims=True)
    second_mean = jnp.mean(grad_hat * normed, axis=-1, keepdims=True)
    return (grad_hat - first_mean - normed * second_mean) * inverse


AXES = ("row", "col")


def exchange(x):
    return lax.all_to_all(x, AXES, split_axis=0, concat_axis=0, tiled=True)


def body(pair, pair_mask, proj_weight, out_weight, in_gain, out_gain, cotangent):
    t = pair.shape[0]
    half_t = t // 2
    channels = pair.shape[2]
    rows = lax.axis_size("row")
    cols = lax.axis_size("col")
    total = t * rows
    half = lax.rem(lax.axis_index("col"), 2)
    normed, inverse = normalize(pair.astype(jnp.float32))
    zn = (normed * in_gain).astype(jnp.bfloat16)
    linear = jnp.einsum("ijc,ce->ije", zn, proj_weight, preferred_element_type=jnp.float32)
    proj_left = linear[..., 0:channels]
    gate_left = linear[..., channels : 2 * channels]
    proj_right = linear[..., 2 * channels : 3 * channels]
    gate_right = linear[..., 3 * channels : 4 * channels]
    gate_out = linear[..., 4 * channels :]
    mask_f = pair_mask.astype(jnp.float32)[..., None]
    sig_left = jax.nn.sigmoid(gate_left)
    sig_right = jax.nn.sigmoid(gate_right)
    left = (mask_f * sig_left * proj_left).astype(jnp.bfloat16)
    right = (mask_f * sig_right * proj_right).astype(jnp.bfloat16)

    def out_full(x):
        x = jnp.transpose(x, (2, 0, 1)).reshape(channels, 1, t * t)
        return jnp.broadcast_to(x, (channels, 2, t * t)).reshape(2 * channels, t * t)

    def matrix(x):
        return (
            x.reshape(rows, cols, t, t).transpose(0, 2, 1, 3).reshape(rows * t, cols * t)
        )

    def pick(x):
        x = x.reshape(x.shape[0], -1, 2, half_t)
        return lax.dynamic_index_in_dim(x, half, 2, keepdims=False).reshape(x.shape[0], -1)

    sent = exchange(jnp.concatenate([out_full(left), out_full(right)], axis=1))
    left_c = matrix(sent[:, : t * t])
    right_c = matrix(sent[:, t * t :])
    tri_c = jnp.einsum("ki,kj->ij", pick(left_c), right_c, preferred_element_type=jnp.float32)
    tri_c = tri_c.astype(jnp.bfloat16).reshape(rows, half_t, cols, t).transpose(0, 2, 1, 3)
    tri = exchange(tri_c.reshape(rows * cols, half_t * t))
    triangle = (
        tri.reshape(channels, 2 * half_t, t).transpose(1, 2, 0).astype(jnp.float32)
    )
    tri_hat, tri_inv = normalize(triangle)
    onorm = (tri_hat * out_gain).astype(jnp.bfloat16)
    projected = jnp.einsum("ijc,cd->ijd", onorm, out_weight, preferred_element_type=jnp.float32)
    sig_gate = jax.nn.sigmoid(gate_out)
    cot_f = cotangent.astype(jnp.float32)
    dproj = (cot_f * sig_gate).astype(jnp.bfloat16)
    dgate = cot_f * projected * sig_gate * (1.0 - sig_gate)
    out_weight_local = jnp.einsum("ijc,ijd->cd", onorm, dproj, preferred_element_type=jnp.float32)
    donorm = jnp.einsum("ijd,cd->ijc", dproj, out_weight, preferred_element_type=jnp.float32)
    out_gain_local = jnp.sum(donorm * tri_hat, axis=(0, 1))
    dtri = layer_back(donorm * out_gain, tri_hat, tri_inv).astype(jnp.bfloat16)
    dtri_c = matrix(exchange(out_full(dtri)))
    dtri_rows = lax.dynamic_index_in_dim(
        dtri_c.reshape(rows, 2, half_t, cols * t), half, 1, keepdims=False
    ).reshape(rows * half_t, cols * t)
    dleft_c = jnp.einsum("kj,ij->ki", right_c, dtri_rows, preferred_element_type=jnp.float32)
    dright_c = jnp.einsum("ki,ij->kj", left_c, pick(dtri_c), preferred_element_type=jnp.float32)

    def back(x):
        x = x.astype(jnp.bfloat16).reshape(rows, t, cols, half_t)
        return x.transpose(0, 2, 1, 3).reshape(rows * cols, t * half_t)

    grads = exchange(jnp.concatenate([back(dleft_c), back(dright_c)], axis=1))

    def cells(x):
        x = x.reshape(channels, 2, t, half_t).transpose(2, 1, 3, 0)
        return x.reshape(t, t, channels).astype(jnp.float32)

    dleft = cells(grads[:, : t * half_t])
    dright = cells(grads[:, t * half_t :])
    dlin = jnp.concatenate(
        [
            dleft * mask_f * sig_left,
            dleft * mask_f * proj_left * sig_left * (1.0 - sig_left),
            dright * mask_f * sig_right,
            dright * mask_f * proj_right * sig_right * (1.0 - sig_right),
            dgate,
        ],
        axis=-1,
    ).astype(jnp.bfloat16)
    proj_local = jnp.einsum("ijc,ije->ce", zn, dlin, preferred_element_type=jnp.float32)
    dzn = jnp.einsum("ije,ce->ijc", dlin, proj_weight, preferred_element_type=jnp.float32)
    in_gain_local = jnp.sum(dzn * normed, axis=(0, 1))
    d_pair = layer_back(dzn * in_gain, normed, inverse)
    proj_sum, out_weight_sum, in_gain_sum, out_gain_sum = lax.psum(
        (proj_local, out_weight_local, in_gain_local, out_gain_local), ("row", "col")
    )
    return (
        d_pair,
        proj_sum / total,
        out_weight_sum / total,
        in_gain_sum / total,
        out_gain_sum / total,
    )


def solution(mesh):
    in_specs = (P("row", "col", None), P("row", "col"), P(), P(), P(), P(), P("row", "col", None))
    out_specs = (P("row", "col", None), P(), P(), P(), P())
    return jax.shard_map(body, mesh=mesh, in_specs=in_specs, out_specs=out_specs, check_vma=False)
```

```python
import jax
import jax.numpy as jnp
from jax import lax
from jax.experimental import pallas as pl
from jax.experimental.pallas import tpu as pltpu
from jax.sharding import PartitionSpec as P


def normalize(values):
    average = jnp.mean(values, axis=-1, keepdims=True)
    centred = values - average
    spread = jnp.mean(centred * centred, axis=-1, keepdims=True)
    inverse = lax.rsqrt(spread + 1e-05)
    return (centred * inverse, inverse)


def layer_back(grad_hat, normed, inverse):
    first_mean = jnp.mean(grad_hat, axis=-1, keepdims=True)
    second_mean = jnp.mean(grad_hat * normed, axis=-1, keepdims=True)
    return (grad_hat - first_mean - normed * second_mean) * inverse


MESH = pl.DeviceIdType.MESH


def settle(ref, sem):
    pltpu.make_async_copy(ref, ref, sem).wait()


def place():
    row = lax.axis_index("row")
    col = lax.axis_index("col")
    return row, col, row * 8 + col // 2, lax.rem(col, 2)


def chip_peer(chip, core):
    return (chip // 8, lax.rem(chip, 8) * 2 + core)


def cell_peer(cell, core):
    return (core * 8 + cell // 16, lax.rem(cell, 16))


def greet(peers, count, own):
    barrier = pltpu.get_barrier_semaphore()

    def step(s, carry):
        row, col, mine = peers(s)

        @pl.when(mine == 0)
        def _():
            pl.semaphore_signal(barrier, inc=1, device_id=(row, col), device_id_type=MESH)

        return carry

    lax.fori_loop(0, count, step, 0)
    pl.semaphore_wait(barrier, count - own)


def spread(x_ref, o_ref, send_sem, recv_sem, to_chip):
    row, col, chip, core = place()
    half = row // 8
    own = 1 - lax.rem(half + core, 2)
    cell = lax.rem(row, 8) * 16 + col
    start, slot = (chip, cell) if to_chip else (cell, chip)

    def is_mine(t, base):
        return jnp.where(t == base, own, 0)

    def toward_chip(s):
        t = lax.rem(chip + s, 128)
        return (*chip_peer(t, half), is_mine(t, chip))

    def toward_cell(s):
        t = lax.rem(cell + s, 128)
        return (*cell_peer(t, core), is_mine(t, cell))

    goes, comes = (toward_chip, toward_cell) if to_chip else (toward_cell, toward_chip)
    greet(comes, 128, own)

    def step(s, carry):
        block = lax.rem(start + s, 128)
        to_row, to_col, mine = goes(s)

        @pl.when(mine == 0)
        def _():
            pltpu.make_async_remote_copy(
                x_ref.at[block],
                o_ref.at[slot],
                send_sem,
                recv_sem,
                device_id=(to_row, to_col),
                device_id_type=MESH,
            ).start()

        @pl.when(mine == 1)
        def _():
            pltpu.make_async_copy(x_ref.at[block], o_ref.at[slot], recv_sem).start()

        return carry

    lax.fori_loop(0, 128, step, 0)
    settle(o_ref, recv_sem)
    settle(x_ref.at[pl.ds(0, 127)], send_sem)

    @pl.when(own == 0)
    def _():
        settle(x_ref.at[0], send_sem)


def transport(x, to_chip, number):
    def kernel(x_ref, o_ref, send_sem, recv_sem):
        spread(x_ref, o_ref, send_sem, recv_sem, to_chip)

    return pl.pallas_call(
        kernel,
        out_shape=jax.ShapeDtypeStruct(x.shape, x.dtype),
        in_specs=[pl.BlockSpec(memory_space=pltpu.VMEM)],
        out_specs=pl.BlockSpec(memory_space=pltpu.VMEM),
        scratch_shapes=[pltpu.SemaphoreType.DMA(()), pltpu.SemaphoreType.DMA(())],
        name=f"transport{number}",
        compiler_params=pltpu.CompilerParams(collective_id=number, has_side_effects=True),
    )(x)


def sum_kernel(x_ref, o_ref, held, send_sem, recv_sem, send_sem2, recv_sem2):
    row, col, _, _ = place()
    me = row * 16 + col
    barrier = pltpu.get_barrier_semaphore()

    def peer(s):
        d = lax.rem(me + s, 256)
        return d, (d // 16, lax.rem(d, 16))

    def hello(s, carry):
        pl.semaphore_signal(barrier, inc=1, device_id=peer(s)[1], device_id_type=MESH)
        return carry

    lax.fori_loop(1, 256, hello, 0)
    pl.semaphore_wait(barrier, 255)

    def scatter(s, carry):
        d, where = peer(s)
        pltpu.make_async_remote_copy(
            x_ref.at[d], held.at[me], send_sem, recv_sem, device_id=where, device_id_type=MESH
        ).start()
        return carry

    pltpu.make_async_copy(x_ref.at[me], held.at[me], recv_sem).start()
    lax.fori_loop(1, 256, scatter, 0)
    settle(held, recv_sem)
    o_ref[me] = jnp.sum(held[...], axis=0)

    def gather(s, carry):
        pltpu.make_async_remote_copy(
            o_ref.at[me], o_ref.at[me], send_sem2, recv_sem2, device_id=peer(s)[1], device_id_type=MESH
        ).start()
        return carry

    lax.fori_loop(1, 256, gather, 0)
    rest = o_ref.at[pl.ds(0, 255)]
    settle(rest, recv_sem2)
    settle(rest, send_sem)
    settle(rest, send_sem2)


def sum_all(x):
    return pl.pallas_call(
        sum_kernel,
        out_shape=jax.ShapeDtypeStruct(x.shape, x.dtype),
        in_specs=[pl.BlockSpec(memory_space=pltpu.VMEM)],
        out_specs=pl.BlockSpec(memory_space=pltpu.VMEM),
        scratch_shapes=[pltpu.VMEM(x.shape, x.dtype)] + [pltpu.SemaphoreType.DMA(())] * 4,
        name="sum_all",
        compiler_params=pltpu.CompilerParams(collective_id=5, has_side_effects=True),
    )(x)


def body(pair, pair_mask, proj_weight, out_weight, in_gain, out_gain, cotangent):
    t = pair.shape[0]
    channels = pair.shape[2]
    rows = lax.axis_size("row")
    cols = lax.axis_size("col")
    total = t * rows
    core = lax.rem(lax.axis_index("col"), 2)
    halves = rows // 2
    partner = [(k, k + 1 - 2 * (k % 2)) for k in range(cols)]
    normed, inverse = normalize(pair.astype(jnp.float32))
    zn = (normed * in_gain).astype(jnp.bfloat16)
    linear = jnp.einsum("ijc,ce->ije", zn, proj_weight, preferred_element_type=jnp.float32)
    proj_left = linear[..., 0:channels]
    gate_left = linear[..., channels : 2 * channels]
    proj_right = linear[..., 2 * channels : 3 * channels]
    gate_right = linear[..., 3 * channels : 4 * channels]
    gate_out = linear[..., 4 * channels :]
    mask_f = pair_mask.astype(jnp.float32)[..., None]
    sig_left = jax.nn.sigmoid(gate_left)
    sig_right = jax.nn.sigmoid(gate_right)
    left = (mask_f * sig_left * proj_left).astype(jnp.bfloat16)
    right = (mask_f * sig_right * proj_right).astype(jnp.bfloat16)

    def by_channel(x):
        return jnp.transpose(x, (2, 0, 1)).reshape(channels, 1, 8, 128)

    def matrix(x):
        x = x.reshape(halves, cols, t, t).transpose(0, 2, 1, 3)
        return x.reshape(halves * t, cols * t)

    def blocks(x):
        x = x.reshape(halves, t, cols, t).transpose(0, 2, 1, 3)
        return x.reshape(halves * cols, 1, 8, 128)

    def to_other(x):
        return lax.ppermute(x, "col", partner)

    def pick(x, index):
        return lax.dynamic_index_in_dim(x.reshape(2, halves * t, cols * t), index, 0, keepdims=False)

    def cells(x):
        return x.reshape(channels, t, t).transpose(1, 2, 0).astype(jnp.float32)

    sent = transport(jnp.concatenate([by_channel(left), by_channel(right)], axis=1), True, 0)
    left_c = matrix(sent[:, 0])
    right_c = matrix(sent[:, 1])
    part = jnp.einsum("ki,kj->ij", left_c, right_c, preferred_element_type=jnp.float32)
    other = to_other(pick(part, 1 - core).astype(jnp.bfloat16)).astype(jnp.float32)
    tri_c = (pick(part, core) + other).astype(jnp.bfloat16)
    triangle = cells(transport(blocks(tri_c), False, 1)[:, 0])
    tri_hat, tri_inv = normalize(triangle)
    onorm = (tri_hat * out_gain).astype(jnp.bfloat16)
    projected = jnp.einsum("ijc,cd->ijd", onorm, out_weight, preferred_element_type=jnp.float32)
    sig_gate = jax.nn.sigmoid(gate_out)
    cot_f = cotangent.astype(jnp.float32)
    dproj = (cot_f * sig_gate).astype(jnp.bfloat16)
    dgate = cot_f * projected * sig_gate * (1.0 - sig_gate)
    out_weight_local = jnp.einsum("ijc,ijd->cd", onorm, dproj, preferred_element_type=jnp.float32)
    donorm = jnp.einsum("ijd,cd->ijc", dproj, out_weight, preferred_element_type=jnp.float32)
    dtri = layer_back(donorm * out_gain, tri_hat, tri_inv).astype(jnp.bfloat16)
    dtri_half = matrix(transport(by_channel(dtri), True, 2)[:, 0])
    dtri_other = to_other(dtri_half)
    dtri_c = jnp.where(
        core == 0,
        jnp.concatenate([dtri_half, dtri_other], axis=0),
        jnp.concatenate([dtri_other, dtri_half], axis=0),
    )
    dleft_c = jnp.einsum("kj,ij->ki", right_c, dtri_c, preferred_element_type=jnp.float32)
    dright_c = jnp.einsum("ki,ij->kj", left_c, dtri_c, preferred_element_type=jnp.float32)
    grads = jnp.concatenate(
        [blocks(dleft_c.astype(jnp.bfloat16)), blocks(dright_c.astype(jnp.bfloat16))], axis=1
    )
    grads = transport(grads, False, 3)
    dleft = cells(grads[:, 0])
    dright = cells(grads[:, 1])
    dlin = jnp.concatenate(
        [
            dleft * mask_f * sig_left,
            dleft * mask_f * proj_left * sig_left * (1.0 - sig_left),
            dright * mask_f * sig_right,
            dright * mask_f * proj_right * sig_right * (1.0 - sig_right),
            dgate,
        ],
        axis=-1,
    ).astype(jnp.bfloat16)
    proj_local = jnp.einsum("ijc,ije->ce", zn, dlin, preferred_element_type=jnp.float32)
    dzn = jnp.einsum("ije,ce->ijc", dlin, proj_weight, preferred_element_type=jnp.float32)
    d_pair = layer_back(dzn * in_gain, normed, inverse)
    sums = sum_all(
        jnp.concatenate([proj_local.reshape(-1, 128), out_weight_local], axis=0).reshape(-1, 3, 128)
    ).reshape(-1, 128)
    scale = 1.0 / total
    d_proj = sums[: channels * 5].reshape(channels, 5 * channels) * scale
    d_out = sums[channels * 5 :] * scale
    d_in_gain = jnp.sum(d_proj * proj_weight.astype(jnp.float32), axis=1) / in_gain
    d_out_gain = jnp.sum(d_out * out_weight.astype(jnp.float32), axis=1) / out_gain
    return (d_pair, d_proj, d_out, d_in_gain, d_out_gain)


def solution(mesh):
    in_specs = (P("row", "col", None), P("row", "col"), P(), P(), P(), P(), P("row", "col", None))
    out_specs = (P("row", "col", None), P(), P(), P(), P())
    return jax.shard_map(body, mesh=mesh, in_specs=in_specs, out_specs=out_specs, check_vma=False)
```

```python
import jax
import jax.numpy as jnp
from jax import lax
from jax.experimental import pallas as pl
from jax.experimental.pallas import tpu as pltpu
from jax.sharding import PartitionSpec as P

MESH = pl.DeviceIdType.MESH
F32 = jnp.float32
BF16 = jnp.bfloat16
EPS = 1e-05


def settle(ref, sem):
    pltpu.make_async_copy(ref, ref, sem).wait()


def device(number):
    return (number // 16, lax.rem(number, 16))


def wrap(value, size):
    return jnp.where(value >= size, value - size, value)


def dot(a, b):
    return jnp.dot(a, b, preferred_element_type=F32)


def dot_nt(a, b):
    return lax.dot_general(a, b, (((1,), (1,)), ((), ())), preferred_element_type=F32)


def dot_tn(a, b):
    return lax.dot_general(a, b, (((0,), (0,)), ((), ())), preferred_element_type=F32)


def mean0(x):
    return jnp.sum(x, axis=0, keepdims=True) * (1.0 / x.shape[0])


def normalize(x):
    centred = x - mean0(x)
    inverse = lax.rsqrt(mean0(centred * centred) + EPS)
    return centred * inverse, inverse


def sigmoid(x):
    return 1.0 / (1.0 + jnp.exp(-x))


def send(src, dst, send_sem, recv_sem, number, me):
    @pl.when(number != me)
    def _():
        pltpu.make_async_remote_copy(
            src, dst, send_sem, recv_sem, device_id=device(number), device_id_type=MESH
        ).start()

    @pl.when(number == me)
    def _():
        pltpu.make_async_copy(src, dst, recv_sem).start()


def kernel(
    pair, mask, w_in, w_out, gain_in, gain_out, cot,
    d_pair, d_w_in, d_w_out, d_gain_in, d_gain_out,
    s1, r1, s2, r2, s3, r3, s4, r4,
    lane_swap, cell_mask, w_in_t, w_out_t, gi, go,
    zhat, s_z, zn, left, right, a_left, b_left, a_right, b_right, gate,
    dproj, upper, h, h_mean, m_left, m_right, part, part_out, part_in,
    tri, onorm, dtri, dtri_f, dtri_all, grad_l, grad_r, dlin,
    g_early, h_early, o_early, a_early, g_late, h_late, o_late, a_late,
    sems,
):
    row = lax.axis_index("row")
    col = lax.axis_index("col")
    me = row * 16 + col
    chip = row * 8 + col // 2
    core = lax.rem(col, 2)
    half = row // 8
    row8 = lax.rem(row, 8)
    cell = row8 * 16 + col
    partner = me + 1 - 2 * core
    own = 1 - lax.rem(half + core, 2)
    scale = 1.0 / 512.0

    barrier = pltpu.get_barrier_semaphore()

    def hello(s, carry):
        pl.semaphore_signal(
            barrier, inc=1, device_id=device(wrap(me + s, 256)), device_id_type=MESH
        )
        return carry

    lax.fori_loop(1, 256, hello, 0)

    def iota(shape, axis):
        return lax.broadcasted_iota(jnp.int32, shape, axis)

    r_i, c_i = iota((128, 128), 0), iota((128, 128), 1)
    to_block = jnp.where(c_i == (r_i & 7) * 16 + (r_i >> 3), 1.0, 0.0).astype(BF16)
    to_tiles = jnp.where(c_i == (r_i & 15) * 8 + (r_i >> 4), 1.0, 0.0).astype(BF16)

    w_in_t[...] = w_in[...].astype(F32).T.astype(BF16)
    w_out_t[...] = w_out[...].astype(F32).T.astype(BF16)
    gi[...] = jnp.broadcast_to(gain_in[...], (128, 128)).T
    go[...] = jnp.broadcast_to(gain_out[...], (128, 128)).T
    spread = jnp.where(iota((32, 128), 0) == (iota((32, 128), 1) & 31), 1.0, 0.0).astype(BF16)
    wide = dot(mask[...].astype(F32).astype(BF16), spread)
    wide = jnp.where((iota((32, 128), 0) >> 3) == (iota((32, 128), 1) >> 5), wide, 0.0)
    wide = wide[0:8] + wide[8:16] + wide[16:24] + wide[24:32]
    for j in range(8):
        cell_mask[j] = wide[j : j + 1]

    def tile(j):
        return pl.ds(pl.multiple_of(j * 128, 128), 128)

    def cells_in(ref, j):
        rows = jnp.concatenate([ref[8 * k + j] for k in range(4)], axis=0)
        return rows.astype(F32).T

    def project(j, carry):
        normed, inverse = normalize(cells_in(pair, j))
        zhat[j] = normed
        s_z[j] = inverse
        z = (normed * gi[...]).astype(BF16)
        zn[:, tile(j)] = z
        keep = cell_mask[j]
        lin = dot(w_in_t[0:256], z)
        sig = sigmoid(lin[128:256])
        value = keep * sig
        product = value * lin[0:128]
        left[j] = product.astype(BF16)
        a_left[j] = value
        b_left[j] = product * (1.0 - sig)
        lin = dot(w_in_t[256:512], z)
        sig = sigmoid(lin[128:256])
        value = keep * sig
        product = value * lin[0:128]
        right[j] = product.astype(BF16)
        a_right[j] = value
        b_right[j] = product * (1.0 - sig)
        return carry

    lax.fori_loop(0, 8, project, 0, unroll=2)

    def to_blocks(src, g):
        return dot(to_block, src[:, 16 * g : 16 * g + 16, :].reshape(128, 128)).reshape(
            16, 8, 128
        ).astype(BF16)

    for g in range(8):
        s1[16 * g : 16 * g + 16, 0] = to_blocks(left, g)
        s1[16 * g : 16 * g + 16, 1] = to_blocks(right, g)

    pl.semaphore_wait(barrier, 255)

    def to_chips(src, dst, k):
        def step(s, carry):
            c = wrap(chip + s, 128)
            send(src.at[c], dst.at[row8, col], sems.at[k], sems.at[k + 1], 2 * c + half, me)
            return carry

        lax.fori_loop(0, 128, step, 0)

    def to_cells(src, dst, k):
        def step(s, carry):
            t = wrap(cell + s, 128)
            send(
                src.at[t // 16, lax.rem(t, 16)], dst.at[chip], sems.at[k], sems.at[k + 1],
                core * 128 + t, me,
            )
            return carry

        lax.fori_loop(0, 128, step, 0)

    def sent(ref, k):
        settle(ref.at[pl.ds(0, 127)], sems.at[k])

        @pl.when(own == 0)
        def _():
            settle(ref.at[0], sems.at[k])

    to_chips(s1, r1, 0)

    l_i, l_o = iota((512, 512), 0), iota((512, 512), 1)
    lane_swap[...] = jnp.where(
        l_o == ((l_i & 96) << 2) + ((l_i >> 7) << 5) + (l_i & 31), 1.0, 0.0
    ).astype(BF16)

    def gates(j, carry):
        z = zn[:, tile(j)]
        sig = sigmoid(dot(w_in_t[512:640], z))
        c_t = cells_in(cot, j)
        c_sig = c_t * sig
        d_p = c_sig.astype(BF16)
        dproj[:, tile(j)] = d_p
        upper[j] = c_sig * (1.0 - sig)
        grad = dot(w_out[...], d_p) * go[...]
        h[j] = grad
        h_mean[j] = mean0(grad)
        return carry

    lax.fori_loop(0, 8, gates, 0, unroll=2)

    def flat(x):
        return x.astype(F32).reshape(64, 128).astype(BF16)

    settle(r1, sems.at[1])

    for side, matrix in ((0, m_left), (1, m_right)):
        for quad in range(4):
            x = jnp.concatenate([flat(r1[:, 4 * quad + k, side]) for k in range(4)], axis=1)
            y = dot(x, lane_swap[...]).astype(BF16)
            for k in range(4):
                matrix[64 * k : 64 * k + 64, 128 * quad : 128 * quad + 128] = y[
                    :, 128 * k : 128 * k + 128
                ]

    def columns(which):
        return m_left[:, pl.ds(pl.multiple_of(which * 256, 256), 256)]

    part_out[...] = dot_tn(columns(1 - core), m_right[...]).astype(BF16)
    swap = pltpu.make_async_remote_copy(
        part_out, part_in, sems.at[2], sems.at[3], device_id=device(partner), device_id_type=MESH
    )
    swap.start()
    part[...] = dot_tn(columns(core), m_right[...])
    swap.wait_recv()
    part[...] = part[...] + part_in[...].astype(F32)
    product = part.reshape(8, 4, 8, 512)

    for quad in range(4):
        lanes = slice(128 * quad, 128 * quad + 128)
        x = jnp.concatenate(
            [product[:, k, :, lanes].reshape(64, 128).astype(BF16) for k in range(4)], axis=1
        )
        y = dot(x, lane_swap[...])
        for k in range(4):
            s2[:, 4 * quad + k] = y[:, 128 * k : 128 * k + 128].reshape(8, 8, 128).astype(BF16)

    to_cells(s2, r2, 4)
    settle(r2, sems.at[5])

    def to_tile_rows(src, dst):
        for g in range(8):
            x = src(g).astype(F32).reshape(128, 128).astype(BF16)
            y = dot(to_tiles, x)
            for j in range(8):
                dst[j, 16 * g : 16 * g + 16, :] = y[16 * j : 16 * j + 16]

    to_tile_rows(lambda g: r2[16 * g : 16 * g + 16], tri)

    def middle(j, carry):
        that, inverse = normalize(tri[j])
        o = (that * go[...]).astype(BF16)
        onorm[:, tile(j)] = o
        dlin[512:640, tile(j)] = (upper[j] * dot(w_out_t[...], o)).astype(BF16)
        grad = h[j]
        d_t = inverse * (grad - h_mean[j] - that * mean0(grad * that))
        dtri[j] = d_t.astype(BF16)
        return carry

    lax.fori_loop(0, 8, middle, 0, unroll=2)

    for g in range(8):
        s3[16 * g : 16 * g + 16] = to_blocks(dtri, g)
    to_chips(s3, r3, 6)

    def fill(dst, base, value):
        for i in range(16):
            dst[base + 2 * i] = value[8 * i : 8 * i + 4]
            dst[base + 2 * i + 1] = value[8 * i + 4 : 8 * i + 8]

    def scatter(src, dst, count, owner, start, k):
        def step(s, carry):
            m = wrap(start + s, count)
            send(src.at[m], dst.at[me], sems.at[k], sems.at[k + 1], owner(m), me)
            return carry

        lax.fori_loop(0, count, step, 0)

    def gather(held, total, dst, m, k):
        total[...] = jnp.sum(held[...], axis=0)

        def step(s, carry):
            send(total, dst.at[m], sems.at[k], sems.at[k + 1], wrap(me + s, 256), me)
            return carry

        lax.fori_loop(0, 256, step, 0)

    fill(g_early, 0, dot_nt(onorm[...], dproj[...]))
    fill(g_early, 32, dot_nt(zn[...], dlin[512:640]))
    early_mine = lax.rem(me, 4) == 3
    scatter(g_early, h_early, 64, lambda m: 4 * m + 3, me // 4, 8)

    settle(r3, sems.at[7])
    for quad in range(4):
        x = jnp.concatenate([flat(r3[:, 4 * quad + k]) for k in range(4)], axis=1)
        y = dot(x, lane_swap[...])
        for k in range(4):
            dtri_f[:, k, :, 128 * quad : 128 * quad + 128] = y[:, 128 * k : 128 * k + 128].reshape(
                8, 8, 128
            )
    dtri_all[core] = dtri_f[...].reshape(256, 512).astype(BF16)
    swap2 = pltpu.make_async_remote_copy(
        dtri_all.at[core], dtri_all.at[core], sems.at[10], sems.at[11],
        device_id=device(partner), device_id_type=MESH,
    )
    swap2.start()
    swap2.wait_recv()
    d_all = dtri_all[...].reshape(512, 512)

    def leave(grad, side):
        for quad in range(4):
            x = jnp.concatenate(
                [
                    grad[64 * k : 64 * k + 64, 128 * quad : 128 * quad + 128]
                    for k in range(4)
                ],
                axis=1,
            )
            y = dot(x, lane_swap[...])
            for k in range(4):
                s4[:, 4 * quad + k, side] = (
                    y[:, 128 * k : 128 * k + 128].reshape(8, 8, 128).astype(BF16)
                )

    leave(dot_nt(m_right[...], d_all).astype(BF16), 0)
    leave(dot(m_left[...], d_all).astype(BF16), 1)
    to_cells(s4, r4, 12)

    @pl.when(early_mine)
    def _():
        settle(h_early, sems.at[9])
        gather(h_early, o_early, a_early, me // 4, 14)

    settle(r4, sems.at[13])
    to_tile_rows(lambda g: r4[16 * g : 16 * g + 16, 0], grad_l)
    to_tile_rows(lambda g: r4[16 * g : 16 * g + 16, 1], grad_r)

    def back(j, carry):
        d_l = grad_l[j]
        d_r = grad_r[j]
        dlin[0:128, tile(j)] = (d_l * a_left[j]).astype(BF16)
        dlin[128:256, tile(j)] = (d_l * b_left[j]).astype(BF16)
        dlin[256:384, tile(j)] = (d_r * a_right[j]).astype(BF16)
        dlin[384:512, tile(j)] = (d_r * b_right[j]).astype(BF16)
        return carry

    lax.fori_loop(0, 8, back, 0, unroll=2)
    sums = dot_nt(zn[...], dlin[0:512])
    for b in range(4):
        fill(g_late, 32 * b, sums[:, 128 * b : 128 * b + 128])
    late_mine = lax.rem(me, 2) == lax.rem(me // 2, 2)
    scatter(g_late, h_late, 128, lambda m: 2 * m + lax.rem(m, 2), chip, 16)

    def finish(j, carry):
        g = dot(w_in[...], dlin[:, tile(j)]) * gi[...]
        normed = zhat[j]
        d = s_z[j] * (g - mean0(g) - normed * mean0(g * normed))
        d = d.T
        for k in range(4):
            d_pair[8 * k + j] = d[32 * k : 32 * k + 32]
        return carry

    lax.fori_loop(0, 8, finish, 0, unroll=2)

    @pl.when(late_mine)
    def _():
        settle(h_late, sems.at[17])
        gather(h_late, o_late, a_late, chip, 18)

    def collect(dst, lanes, src, base):
        for i in range(16):
            dst[8 * i : 8 * i + 4, lanes] = src[base + 2 * i] * scale
            dst[8 * i + 4 : 8 * i + 8, lanes] = src[base + 2 * i + 1] * scale

    settle(a_early, sems.at[15])
    collect(d_w_out, slice(0, 128), a_early, 0)
    collect(d_w_in, slice(512, 640), a_early, 32)
    settle(a_late, sems.at[19])
    for b in range(4):
        collect(d_w_in, slice(128 * b, 128 * b + 128), a_late, 32 * b)
    weighted = d_w_in[...] * w_in[...].astype(F32)
    folded = weighted[:, 0:128]
    for b in range(1, 5):
        folded = folded + weighted[:, 128 * b : 128 * b + 128]
    d_gain_in[...] = jnp.sum(folded.T, axis=0, keepdims=True) / gain_in[...]
    weighted = d_w_out[...] * w_out[...].astype(F32)
    d_gain_out[...] = jnp.sum(weighted.T, axis=0, keepdims=True) / gain_out[...]

    sent(s1, 0)
    swap.wait_send()
    flat_sent = ((r2, 4), (s3, 6), (r4, 12))
    for ref, k in flat_sent:
        sent(ref, k)
    swap2.wait_send()
    settle(g_early.at[pl.ds(0, 63)], sems.at[8])

    @pl.when(jnp.logical_not(early_mine))
    def _():
        settle(g_early.at[0], sems.at[8])

    @pl.when(early_mine)
    def _():
        settle(h_early.at[pl.ds(0, 255)], sems.at[14])

    settle(g_late.at[pl.ds(0, 127)], sems.at[16])

    @pl.when(jnp.logical_not(late_mine))
    def _():
        settle(g_late.at[0], sems.at[16])

    @pl.when(late_mine)
    def _():
        settle(h_late.at[pl.ds(0, 255)], sems.at[18])


def body(pair, pair_mask, proj_weight, out_weight, in_gain, out_gain, cotangent):
    vmem = pl.BlockSpec(memory_space=pltpu.VMEM)
    V = pltpu.VMEM
    tiles = V((8, 128, 128), F32)
    tiles16 = V((8, 128, 128), BF16)
    by_tile = V((8, 1, 128), F32)
    lanes16 = V((128, 1024), BF16)
    scratch = [
        V((128, 2, 8, 128), BF16), V((8, 16, 2, 8, 128), BF16),
        V((8, 16, 8, 128), BF16), V((128, 8, 128), BF16),
        V((128, 8, 128), BF16), V((8, 16, 8, 128), BF16),
        V((8, 16, 2, 8, 128), BF16), V((128, 2, 8, 128), BF16),
        V((512, 512), BF16), by_tile, V((640, 128), BF16), V((128, 128), BF16),
        V((128, 128), F32), V((128, 128), F32),
        tiles, by_tile, lanes16, tiles16, tiles16, tiles, tiles, tiles, tiles, V((8, 128), F32),
        lanes16, tiles, tiles, by_tile, V((256, 512), BF16), V((256, 512), BF16),
        V((256, 512), F32), V((256, 512), BF16), V((256, 512), BF16),
        tiles, lanes16, tiles16, V((8, 4, 8, 512), F32), V((2, 256, 512), BF16),
        tiles, tiles, V((640, 1024), BF16),
        V((64, 4, 128), F32), V((256, 4, 128), F32), V((4, 128), F32), V((64, 4, 128), F32),
        V((128, 4, 128), F32), V((256, 4, 128), F32), V((4, 128), F32), V((128, 4, 128), F32),
        pltpu.SemaphoreType.DMA((20,)),
    ]
    outs = pl.pallas_call(
        kernel,
        out_shape=(
            jax.ShapeDtypeStruct(pair.shape, F32),
            jax.ShapeDtypeStruct((128, 640), F32),
            jax.ShapeDtypeStruct((128, 128), F32),
            jax.ShapeDtypeStruct((1, 128), F32),
            jax.ShapeDtypeStruct((1, 128), F32),
        ),
        in_specs=[vmem] * 7,
        out_specs=[vmem] * 5,
        scratch_shapes=scratch,
        name="triangle_back",
        compiler_params=pltpu.CompilerParams(collective_id=0, has_side_effects=True),
    )(
        pair, pair_mask, proj_weight, out_weight,
        in_gain.reshape(1, 128), out_gain.reshape(1, 128), cotangent,
    )
    return (*outs[:3], outs[3].reshape(128), outs[4].reshape(128))


def solution(mesh):
    in_specs = (P("row", "col", None), P("row", "col"), P(), P(), P(), P(), P("row", "col", None))
    out_specs = (P("row", "col", None), P(), P(), P(), P())
    return jax.shard_map(body, mesh=mesh, in_specs=in_specs, out_specs=out_specs, check_vma=False)
```

```python
import jax
import jax.numpy as jnp
from jax import lax
from jax.experimental import pallas as pl
from jax.experimental.pallas import tpu as pltpu
from jax.sharding import PartitionSpec as P

MESH = pl.DeviceIdType.MESH
F32 = jnp.float32
BF16 = jnp.bfloat16
EPS = 1e-05


def settle(ref, sem):
    pltpu.make_async_copy(ref, ref, sem).wait()


def wrap(value, size):
    return jnp.where(value >= size, value - size, value)


def dot(a, b):
    return jnp.dot(a, b, preferred_element_type=F32)


def dot_nt(a, b):
    return lax.dot_general(a, b, (((1,), (1,)), ((), ())), preferred_element_type=F32)


def dot_tn(a, b):
    return lax.dot_general(a, b, (((0,), (0,)), ((), ())), preferred_element_type=F32)


def mean0(x):
    return jnp.sum(x, axis=0, keepdims=True) * (1.0 / x.shape[0])


def normalize(x):
    centred = x - mean0(x)
    inverse = lax.rsqrt(mean0(centred * centred) + EPS)
    return centred * inverse, inverse


def sigmoid(x):
    return 1.0 / (1.0 + jnp.exp(-x))


def start(src, dst, send_sem, recv_sem, row, col):
    pltpu.make_async_remote_copy(
        src, dst, send_sem, recv_sem, device_id=(row, col), device_id_type=MESH
    ).start()


def keep_or_start(mine, src, dst, send_sem, recv_sem, row, col):
    @pl.when(mine)
    def _():
        pltpu.make_async_copy(src, dst, recv_sem).start()

    @pl.when(jnp.logical_not(mine))
    def _():
        start(src, dst, send_sem, recv_sem, row, col)


def kernel(
    pair, mask, w_in, w_out, gain_in, gain_out, cot,
    d_pair, d_w_in, d_w_out, d_gain_in, d_gain_out,
    s1, r1, s2, r2, s3, r3, s4l, s4r, r4l, r4r,
    lane_swap, cell_mask, w_in_t, w_out_t, gi, go,
    zhat, s_z, zn, left, right, a_left, b_left, a_right, b_right, gate,
    dproj, upper, h, h_mean, m_left, m_right, part, part_out, part_in,
    tri, onorm, dtri, dtri_f, dtri_all, grad_l, grad_r, dlin,
    g_early, h_early, o_early, a_early, g_l, h_l, o_l, a_l, g_r, h_r, o_r, a_r,
    sems,
):
    row = lax.axis_index("row")
    col = lax.axis_index("col")
    me = row * 16 + col
    chip = row * 8 + col // 2
    core = lax.rem(col, 2)
    half = row // 8
    row8 = lax.rem(row, 8)
    cell = row8 * 16 + col
    seat = col // 2
    beside = (row, col + 1 - 2 * core)
    mine = half == core
    scale = 1.0 / 512.0
    barrier = pltpu.get_barrier_semaphore()

    def hello(a, first=0):
        to_row = wrap(row + a, 16)
        for b in range(first, 16):
            pl.semaphore_signal(
                barrier, inc=1, device_id=(to_row, wrap(col + b, 16)), device_id_type=MESH
            )

    def hello_row(a, carry):
        hello(a)
        return carry

    lax.fori_loop(7, 16, hello_row, 0)
    lax.fori_loop(1, 7, hello_row, 0)
    hello(0, 1)

    def iota(shape, axis):
        return lax.broadcasted_iota(jnp.int32, shape, axis)

    r_i, c_i = iota((128, 128), 0), iota((128, 128), 1)
    to_block = jnp.where(c_i == (r_i & 7) * 16 + (r_i >> 3), 1.0, 0.0).astype(BF16)
    to_tiles = jnp.where(c_i == (r_i & 15) * 8 + (r_i >> 4), 1.0, 0.0).astype(BF16)

    w_in_t[...] = w_in[...].astype(F32).T.astype(BF16)
    w_out_t[...] = w_out[...].astype(F32).T.astype(BF16)
    gi[...] = jnp.broadcast_to(gain_in[...], (128, 128)).T
    go[...] = jnp.broadcast_to(gain_out[...], (128, 128)).T
    spread = jnp.where(iota((32, 128), 0) == (iota((32, 128), 1) & 31), 1.0, 0.0).astype(BF16)
    wide = dot(mask[...].astype(F32).astype(BF16), spread)
    wide = jnp.where((iota((32, 128), 0) >> 3) == (iota((32, 128), 1) >> 5), wide, 0.0)
    wide = wide[0:8] + wide[8:16] + wide[16:24] + wide[24:32]
    for j in range(8):
        cell_mask[j] = wide[j : j + 1]

    def tile(j):
        return pl.ds(pl.multiple_of(j * 128, 128), 128)

    def cells_in(ref, j):
        rows = jnp.concatenate([ref[8 * k + j] for k in range(4)], axis=0)
        return rows.astype(F32).T

    def project(j, carry):
        normed, inverse = normalize(cells_in(pair, j))
        zhat[j] = normed
        s_z[j] = inverse
        z = (normed * gi[...]).astype(BF16)
        zn[:, tile(j)] = z
        keep = cell_mask[j]
        lin = dot(w_in_t[0:256], z)
        sig = sigmoid(lin[128:256])
        value = keep * sig
        product = value * lin[0:128]
        left[j] = product.astype(BF16)
        a_left[j] = value
        b_left[j] = product * (1.0 - sig)
        lin = dot(w_in_t[256:512], z)
        sig = sigmoid(lin[128:256])
        value = keep * sig
        product = value * lin[0:128]
        right[j] = product.astype(BF16)
        a_right[j] = value
        b_right[j] = product * (1.0 - sig)
        return carry

    lax.fori_loop(0, 8, project, 0, unroll=2)

    def to_blocks(src, g):
        return dot(to_block, src[:, 16 * g : 16 * g + 16, :].reshape(128, 128)).reshape(
            16, 8, 128
        ).astype(BF16)

    for g in range(8):
        s1[16 * g : 16 * g + 16, 0] = to_blocks(left, g)
        s1[16 * g : 16 * g + 16, 1] = to_blocks(right, g)

    pl.semaphore_wait(barrier, 255)

    def to_chips(src, dst, k):
        there = dst.at[row8, col]

        def ring(a, first=0):
            to_row = wrap(row + a, 16)
            for b in range(first, 8):
                to_seat = wrap(seat + b, 8)
                start(
                    src.at[to_row * 8 + to_seat], there, sems.at[k], sems.at[k + 1],
                    to_row, 2 * to_seat + half,
                )

        def step(a, carry):
            ring(a)
            return carry

        keep_or_start(mine, src.at[chip], there, sems.at[k], sems.at[k + 1], *beside)
        ring(0, 1)
        lax.fori_loop(1, 16, step, 0)

    def to_cells(src, dst, k):
        there = dst.at[chip]
        base = core * 8

        def ring(a, first=0):
            block = wrap(row8 + a, 8)
            for b in range(first, 16):
                to_col = wrap(col + b, 16)
                start(
                    src.at[block, to_col], there, sems.at[k], sems.at[k + 1],
                    base + block, to_col,
                )

        def step(a, carry):
            ring(a)
            return carry

        keep_or_start(
            mine, src.at[row8, col], there, sems.at[k], sems.at[k + 1], base + row8, col
        )
        ring(0, 1)
        lax.fori_loop(1, 8, step, 0)

    def sent(ref, k):
        settle(ref.at[pl.ds(0, 127)], sems.at[k])

        @pl.when(jnp.logical_not(mine))
        def _():
            settle(ref.at[0], sems.at[k])

    to_chips(s1, r1, 0)

    l_i, l_o = iota((512, 512), 0), iota((512, 512), 1)
    lane_swap[...] = jnp.where(
        l_o == ((l_i & 96) << 2) + ((l_i >> 7) << 5) + (l_i & 31), 1.0, 0.0
    ).astype(BF16)

    def gates(j, carry):
        z = zn[:, tile(j)]
        sig = sigmoid(dot(w_in_t[512:640], z))
        c_t = cells_in(cot, j)
        c_sig = c_t * sig
        d_p = c_sig.astype(BF16)
        dproj[:, tile(j)] = d_p
        upper[j] = c_sig * (1.0 - sig)
        grad = dot(w_out[...], d_p) * go[...]
        h[j] = grad
        h_mean[j] = mean0(grad)
        return carry

    lax.fori_loop(0, 8, gates, 0, unroll=2)

    def flat(x):
        return x.astype(F32).reshape(64, 128).astype(BF16)

    settle(r1, sems.at[1])

    for side, matrix in ((0, m_left), (1, m_right)):
        for quad in range(4):
            x = jnp.concatenate([flat(r1[:, 4 * quad + k, side]) for k in range(4)], axis=1)
            y = dot(x, lane_swap[...]).astype(BF16)
            for k in range(4):
                matrix[64 * k : 64 * k + 64, 128 * quad : 128 * quad + 128] = y[
                    :, 128 * k : 128 * k + 128
                ]

    def columns(which):
        return m_left[:, pl.ds(pl.multiple_of(which * 256, 256), 256)]

    part_out[...] = dot_tn(columns(1 - core), m_right[...]).astype(BF16)
    swap = pltpu.make_async_remote_copy(
        part_out, part_in, sems.at[2], sems.at[3], device_id=beside, device_id_type=MESH
    )
    swap.start()
    part[...] = dot_tn(columns(core), m_right[...])
    swap.wait_recv()
    part[...] = part[...] + part_in[...].astype(F32)
    product = part.reshape(8, 4, 8, 512)

    for quad in range(4):
        lanes = slice(128 * quad, 128 * quad + 128)
        x = jnp.concatenate(
            [product[:, k, :, lanes].reshape(64, 128).astype(BF16) for k in range(4)], axis=1
        )
        y = dot(x, lane_swap[...])
        for k in range(4):
            s2[:, 4 * quad + k] = y[:, 128 * k : 128 * k + 128].reshape(8, 8, 128).astype(BF16)

    to_cells(s2, r2, 4)
    settle(r2, sems.at[5])

    def to_tile_rows(src, dst):
        for g in range(8):
            x = src(g).astype(F32).reshape(128, 128).astype(BF16)
            y = dot(to_tiles, x)
            for j in range(8):
                dst[j, 16 * g : 16 * g + 16, :] = y[16 * j : 16 * j + 16]

    to_tile_rows(lambda g: r2[16 * g : 16 * g + 16], tri)

    def middle(j, carry):
        that, inverse = normalize(tri[j])
        o = (that * go[...]).astype(BF16)
        onorm[:, tile(j)] = o
        dlin[512:640, tile(j)] = (upper[j] * dot(w_out_t[...], o)).astype(BF16)
        grad = h[j]
        d_t = inverse * (grad - h_mean[j] - that * mean0(grad * that))
        dtri[j] = d_t.astype(BF16)
        return carry

    lax.fori_loop(0, 8, middle, 0, unroll=2)

    for g in range(8):
        s3[16 * g : 16 * g + 16] = to_blocks(dtri, g)
    to_chips(s3, r3, 6)

    def fill(dst, value):
        rows = value.astype(BF16)
        for b in range(2):
            for i in range(64):
                dst[64 * b + i] = rows[2 * i : 2 * i + 2, 128 * b : 128 * b + 128]

    def owner(to_seat, flip):
        return lax.rem(to_seat + flip, 2)

    def scatter(src, dst, flip, k):
        there = dst.at[me]

        def ring(a, first=0):
            to_row = wrap(row + a, 16)
            for b in range(first, 8):
                to_seat = wrap(seat + b, 8)
                start(
                    src.at[to_row * 8 + to_seat], there, sems.at[k], sems.at[k + 1],
                    to_row, 2 * to_seat + owner(to_seat, flip),
                )

        def step(a, carry):
            ring(a)
            return carry

        keep_or_start(
            owner(seat, flip) == core, src.at[chip], there, sems.at[k], sems.at[k + 1], *beside
        )
        ring(0, 1)
        lax.fori_loop(1, 16, step, 0)

    def gather(held, total, dst, flip, k):
        @pl.when(owner(seat, flip) == core)
        def _():
            settle(held, sems.at[k + 1])
            total[...] = jnp.sum(held[...].astype(F32), axis=0).astype(BF16)
            there = dst.at[chip]

            def ring(a, first=0):
                to_row = wrap(row + a, 16)
                for b in range(first, 16):
                    start(
                        total, there, sems.at[k + 2], sems.at[k + 3],
                        to_row, wrap(col + b, 16),
                    )

            def step(a, carry):
                ring(a)
                return carry

            pltpu.make_async_copy(total, there, sems.at[k + 3]).start()
            ring(0, 1)
            lax.fori_loop(1, 16, step, 0)

    def finished(src, held, flip, k):
        settle(src.at[pl.ds(0, 127)], sems.at[k])

        @pl.when(owner(seat, flip) != core)
        def _():
            settle(src.at[0], sems.at[k])

        @pl.when(owner(seat, flip) == core)
        def _():
            settle(held.at[pl.ds(0, 255)], sems.at[k + 2])

    fill(
        g_early,
        jnp.concatenate(
            [dot_nt(onorm[...], dproj[...]), dot_nt(zn[...], dlin[512:640])], axis=1
        ),
    )

    settle(r3, sems.at[7])
    for quad in range(4):
        x = jnp.concatenate([flat(r3[:, 4 * quad + k]) for k in range(4)], axis=1)
        y = dot(x, lane_swap[...])
        for k in range(4):
            dtri_f[:, k, :, 128 * quad : 128 * quad + 128] = y[:, 128 * k : 128 * k + 128].reshape(
                8, 8, 128
            )
    dtri_all[core] = dtri_f[...].reshape(256, 512).astype(BF16)
    swap2 = pltpu.make_async_remote_copy(
        dtri_all.at[core], dtri_all.at[core], sems.at[10], sems.at[11],
        device_id=beside, device_id_type=MESH,
    )
    swap2.start()
    swap2.wait_recv()
    d_all = dtri_all[...].reshape(512, 512)

    def leave(grad, dst):
        for quad in range(4):
            x = jnp.concatenate(
                [
                    grad[64 * k : 64 * k + 64, 128 * quad : 128 * quad + 128]
                    for k in range(4)
                ],
                axis=1,
            )
            y = dot(x, lane_swap[...])
            for k in range(4):
                dst[:, 4 * quad + k] = (
                    y[:, 128 * k : 128 * k + 128].reshape(8, 8, 128).astype(BF16)
                )

    leave(dot_nt(m_right[...], d_all).astype(BF16), s4l)
    to_cells(s4l, r4l, 12)
    leave(dot(m_left[...], d_all).astype(BF16), s4r)
    to_cells(s4r, r4r, 14)
    scatter(g_early, h_early, 1, 16)

    def back(grad, value, slope, base):
        def step(j, carry):
            d = grad[j]
            dlin[base : base + 128, tile(j)] = (d * value[j]).astype(BF16)
            dlin[base + 128 : base + 256, tile(j)] = (d * slope[j]).astype(BF16)
            return carry

        lax.fori_loop(0, 8, step, 0, unroll=2)

    settle(r4l, sems.at[13])
    to_tile_rows(lambda g: r4l[16 * g : 16 * g + 16], grad_l)
    back(grad_l, a_left, b_left, 0)
    fill(g_l, dot_nt(zn[...], dlin[0:256]))
    scatter(g_l, h_l, 0, 20)

    settle(r4r, sems.at[15])
    to_tile_rows(lambda g: r4r[16 * g : 16 * g + 16], grad_r)
    back(grad_r, a_right, b_right, 256)
    fill(g_r, dot_nt(zn[...], dlin[256:512]))
    scatter(g_r, h_r, 1, 24)

    gather(h_early, o_early, a_early, 1, 16)
    gather(h_l, o_l, a_l, 0, 20)

    def finish(j, carry):
        g = dot(w_in[...], dlin[:, tile(j)]) * gi[...]
        normed = zhat[j]
        d = s_z[j] * (g - mean0(g) - normed * mean0(g * normed))
        d = d.T
        for k in range(4):
            d_pair[8 * k + j] = d[32 * k : 32 * k + 32]
        return carry

    lax.fori_loop(0, 4, finish, 0, unroll=2)
    gather(h_r, o_r, a_r, 1, 24)
    lax.fori_loop(4, 8, finish, 0, unroll=2)

    def collect(dst, lanes, src, base):
        for i in range(64):
            dst[2 * i : 2 * i + 2, lanes] = src[base + i].astype(F32) * scale

    settle(a_early, sems.at[19])
    collect(d_w_out, slice(0, 128), a_early, 0)
    collect(d_w_in, slice(512, 640), a_early, 64)
    weighted = d_w_out[...] * w_out[...].astype(F32)
    d_gain_out[...] = jnp.sum(weighted.T, axis=0, keepdims=True) / gain_out[...]
    settle(a_l, sems.at[23])
    collect(d_w_in, slice(0, 128), a_l, 0)
    collect(d_w_in, slice(128, 256), a_l, 64)
    settle(a_r, sems.at[27])
    collect(d_w_in, slice(256, 384), a_r, 0)
    collect(d_w_in, slice(384, 512), a_r, 64)
    weighted = d_w_in[...] * w_in[...].astype(F32)
    folded = weighted[:, 0:128]
    for b in range(1, 5):
        folded = folded + weighted[:, 128 * b : 128 * b + 128]
    d_gain_in[...] = jnp.sum(folded.T, axis=0, keepdims=True) / gain_in[...]

    sent(s1, 0)
    swap.wait_send()
    sent(r2, 4)
    sent(s3, 6)
    swap2.wait_send()
    sent(r4l, 12)
    sent(r4r, 14)
    finished(g_early, h_early, 1, 16)
    finished(g_l, h_l, 0, 20)
    finished(g_r, h_r, 1, 24)


def body(pair, pair_mask, proj_weight, out_weight, in_gain, out_gain, cotangent):
    vmem = pl.BlockSpec(memory_space=pltpu.VMEM)
    V = pltpu.VMEM
    tiles = V((8, 128, 128), F32)
    tiles16 = V((8, 128, 128), BF16)
    by_tile = V((8, 1, 128), F32)
    lanes16 = V((128, 1024), BF16)
    sums = (V((128, 2, 128), BF16), V((256, 2, 128), BF16), V((2, 128), BF16), V((128, 2, 128), BF16))
    scratch = [
        V((128, 2, 8, 128), BF16), V((8, 16, 2, 8, 128), BF16),
        V((8, 16, 8, 128), BF16), V((128, 8, 128), BF16),
        V((128, 8, 128), BF16), V((8, 16, 8, 128), BF16),
        V((8, 16, 8, 128), BF16), V((8, 16, 8, 128), BF16),
        V((128, 8, 128), BF16), V((128, 8, 128), BF16),
        V((512, 512), BF16), by_tile, V((640, 128), BF16), V((128, 128), BF16),
        V((128, 128), F32), V((128, 128), F32),
        tiles, by_tile, lanes16, tiles16, tiles16, tiles, tiles, tiles, tiles, V((8, 128), F32),
        lanes16, tiles, tiles, by_tile, V((256, 512), BF16), V((256, 512), BF16),
        V((256, 512), F32), V((256, 512), BF16), V((256, 512), BF16),
        tiles, lanes16, tiles16, V((8, 4, 8, 512), F32), V((2, 256, 512), BF16),
        tiles, tiles, V((640, 1024), BF16),
        *sums, *sums, *sums,
        pltpu.SemaphoreType.DMA((28,)),
    ]
    outs = pl.pallas_call(
        kernel,
        out_shape=(
            jax.ShapeDtypeStruct(pair.shape, F32),
            jax.ShapeDtypeStruct((128, 640), F32),
            jax.ShapeDtypeStruct((128, 128), F32),
            jax.ShapeDtypeStruct((1, 128), F32),
            jax.ShapeDtypeStruct((1, 128), F32),
        ),
        in_specs=[vmem] * 7,
        out_specs=[vmem] * 5,
        scratch_shapes=scratch,
        name="triangle_back",
        compiler_params=pltpu.CompilerParams(collective_id=0, has_side_effects=True),
    )(
        pair, pair_mask, proj_weight, out_weight,
        in_gain.reshape(1, 128), out_gain.reshape(1, 128), cotangent,
    )
    return (*outs[:3], outs[3].reshape(128), outs[4].reshape(128))


def solution(mesh):
    in_specs = (P("row", "col", None), P("row", "col"), P(), P(), P(), P(), P("row", "col", None))
    out_specs = (P("row", "col", None), P(), P(), P(), P())
    return jax.shard_map(body, mesh=mesh, in_specs=in_specs, out_specs=out_specs, check_vma=False)
```

```python
import jax
import jax.numpy as jnp
from jax import lax
from jax.experimental import pallas as pl
from jax.experimental.pallas import tpu as pltpu
from jax.sharding import PartitionSpec as P

MESH = pl.DeviceIdType.MESH
F32 = jnp.float32
BF16 = jnp.bfloat16
EPS = 1e-05


def settle(ref, sem):
    pltpu.make_async_copy(ref, ref, sem).wait()


def wrap(value, size):
    return jnp.where(value >= size, value - size, value)


def dot(a, b):
    return jnp.dot(a, b, preferred_element_type=F32)


def dot_nt(a, b):
    return lax.dot_general(a, b, (((1,), (1,)), ((), ())), preferred_element_type=F32)


def dot_tn(a, b):
    return lax.dot_general(a, b, (((0,), (0,)), ((), ())), preferred_element_type=F32)


def mean0(x):
    return jnp.sum(x, axis=0, keepdims=True) * (1.0 / x.shape[0])


def normalize(x):
    centred = x - mean0(x)
    inverse = lax.rsqrt(mean0(centred * centred) + EPS)
    return centred * inverse, inverse


def sigmoid(x):
    return 1.0 / (1.0 + jnp.exp(-x))


def start(src, dst, send_sem, recv_sem, row, col):
    pltpu.make_async_remote_copy(
        src, dst, send_sem, recv_sem, device_id=(row, col), device_id_type=MESH
    ).start()


def keep_or_start(mine, src, dst, send_sem, recv_sem, row, col):
    @pl.when(mine)
    def _():
        pltpu.make_async_copy(src, dst, recv_sem).start()

    @pl.when(jnp.logical_not(mine))
    def _():
        start(src, dst, send_sem, recv_sem, row, col)


def kernel(
    pair_h, mask_h, w_in_h, w_out_h, gain_in_h, gain_out_h, cot_h,
    d_pair_h, d_w_in, d_w_out, d_gain_in, d_gain_out,
    s1l, s1r, r1l, r1r, s2, r2, s3, r3, s4l, s4r, r4l, r4r,
    lane_swap, cell_mask, w_in_t, w_out_t, gi, go,
    zhat, s_z, zn, left, right, a_left, b_left, a_right, b_right,
    dproj, upper, h, h_mean, m_left, m_right, part, part_out, part_in,
    tri, onorm, dtri, dtri_f, dtri_all, grad_l, grad_r, dlin,
    g_early, h_early, o_early, a_early, g_l, h_l, o_l, a_l, g_r, h_r, o_r, a_r,
    pair, mask, w_in, w_out, gain_in, gain_out, cot, d_pair,
    local_sems, sems,
):
    row = lax.axis_index("row")
    col = lax.axis_index("col")
    me = row * 16 + col
    chip = row * 8 + col // 2
    core = lax.rem(col, 2)
    half = row // 8
    row8 = lax.rem(row, 8)
    cell = row8 * 16 + col
    seat = col // 2
    beside = (row, col + 1 - 2 * core)
    mine = half == core
    scale = 1.0 / 512.0
    loads = [
        pltpu.make_async_copy(src, dst, local_sems.at[n])
        for n, (src, dst) in enumerate(
            (
                (w_in_h, w_in), (w_out_h, w_out), (gain_in_h, gain_in), (gain_out_h, gain_out),
                (mask_h, mask), (pair_h, pair), (cot_h, cot),
            )
        )
    ]
    for load in loads:
        load.start()
    barrier = pltpu.get_barrier_semaphore()

    def hello(a, first=0):
        to_row = wrap(row + a, 16)
        for b in range(first, 16):
            pl.semaphore_signal(
                barrier, inc=1, device_id=(to_row, wrap(col + b, 16)), device_id_type=MESH
            )

    def hello_row(a, carry):
        hello(a)
        return carry

    lax.fori_loop(7, 16, hello_row, 0)
    lax.fori_loop(1, 7, hello_row, 0)
    hello(0, 1)

    def iota(shape, axis):
        return lax.broadcasted_iota(jnp.int32, shape, axis)

    r_i, c_i = iota((128, 128), 0), iota((128, 128), 1)
    to_block = jnp.where(c_i == (r_i & 7) * 16 + (r_i >> 3), 1.0, 0.0).astype(BF16)
    to_tiles = jnp.where(c_i == (r_i & 15) * 8 + (r_i >> 4), 1.0, 0.0).astype(BF16)

    for load in loads[:6]:
        load.wait()
    w_in_t[...] = w_in[...].astype(F32).T.astype(BF16)
    w_out_t[...] = w_out[...].astype(F32).T.astype(BF16)
    gi[...] = jnp.broadcast_to(gain_in[...], (128, 128)).T
    go[...] = jnp.broadcast_to(gain_out[...], (128, 128)).T
    spread = jnp.where(iota((32, 128), 0) == (iota((32, 128), 1) & 31), 1.0, 0.0).astype(BF16)
    wide = dot(mask[...].astype(F32).astype(BF16), spread)
    wide = jnp.where((iota((32, 128), 0) >> 3) == (iota((32, 128), 1) >> 5), wide, 0.0)
    wide = wide[0:8] + wide[8:16] + wide[16:24] + wide[24:32]
    for j in range(8):
        cell_mask[j] = wide[j : j + 1]

    def tile(j):
        return pl.ds(pl.multiple_of(j * 128, 128), 128)

    def cells_in(ref, j):
        rows = jnp.concatenate([ref[8 * k + j] for k in range(4)], axis=0)
        return rows.astype(F32).T

    def project(j, carry):
        normed, inverse = normalize(cells_in(pair, j))
        zhat[j] = normed
        s_z[j] = inverse
        z = (normed * gi[...]).astype(BF16)
        zn[:, tile(j)] = z
        keep = cell_mask[j]
        lin = dot(w_in_t[0:256], z)
        sig = sigmoid(lin[128:256])
        value = keep * sig
        product = value * lin[0:128]
        left[j] = product.astype(BF16)
        a_left[j] = value
        b_left[j] = product * (1.0 - sig)
        lin = dot(w_in_t[256:512], z)
        sig = sigmoid(lin[128:256])
        value = keep * sig
        product = value * lin[0:128]
        right[j] = product.astype(BF16)
        a_right[j] = value
        b_right[j] = product * (1.0 - sig)
        return carry

    lax.fori_loop(0, 8, project, 0, unroll=2)

    def to_blocks(src, g):
        return dot(to_block, src[:, 16 * g : 16 * g + 16, :].reshape(128, 128)).reshape(
            16, 8, 128
        ).astype(BF16)

    for g in range(8):
        s1l[16 * g : 16 * g + 16] = to_blocks(left, g)
        s1r[16 * g : 16 * g + 16] = to_blocks(right, g)

    pl.semaphore_wait(barrier, 255)

    def to_chips(src, dst, k):
        there = dst.at[row8, col]

        def ring(a, first=0):
            to_row = wrap(row + a, 16)
            for b in range(first, 8):
                to_seat = wrap(seat + b, 8)
                start(
                    src.at[to_row * 8 + to_seat], there, sems.at[k], sems.at[k + 1],
                    to_row, 2 * to_seat + half,
                )

        def step(a, carry):
            ring(a)
            return carry

        keep_or_start(mine, src.at[chip], there, sems.at[k], sems.at[k + 1], *beside)
        ring(0, 1)
        lax.fori_loop(1, 16, step, 0)

    def to_cells(src, dst, k):
        there = dst.at[chip]
        base = core * 8

        def ring(a, first=0):
            block = wrap(row8 + a, 8)
            for b in range(first, 16):
                to_col = wrap(col + b, 16)
                start(
                    src.at[block, to_col], there, sems.at[k], sems.at[k + 1],
                    base + block, to_col,
                )

        def step(a, carry):
            ring(a)
            return carry

        keep_or_start(
            mine, src.at[row8, col], there, sems.at[k], sems.at[k + 1], base + row8, col
        )
        ring(0, 1)
        lax.fori_loop(1, 8, step, 0)

    def sent(ref, k):
        settle(ref.at[pl.ds(0, 127)], sems.at[k])

        @pl.when(jnp.logical_not(mine))
        def _():
            settle(ref.at[0], sems.at[k])

    to_chips(s1l, r1l, 0)
    to_chips(s1r, r1r, 28)

    l_i, l_o = iota((512, 512), 0), iota((512, 512), 1)
    lane_swap[...] = jnp.where(
        l_o == ((l_i & 96) << 2) + ((l_i >> 7) << 5) + (l_i & 31), 1.0, 0.0
    ).astype(BF16)

    def gates(j, carry):
        z = zn[:, tile(j)]
        sig = sigmoid(dot(w_in_t[512:640], z))
        c_t = cells_in(cot, j)
        c_sig = c_t * sig
        d_p = c_sig.astype(BF16)
        dproj[:, tile(j)] = d_p
        upper[j] = c_sig * (1.0 - sig)
        grad = dot(w_out[...], d_p) * go[...]
        h[j] = grad
        h_mean[j] = mean0(grad)
        return carry

    loads[6].wait()
    lax.fori_loop(0, 8, gates, 0, unroll=2)

    def flat(x):
        return x.astype(F32).reshape(64, 128).astype(BF16)

    def swapped(piece):
        x = jnp.concatenate(
            [
                jnp.concatenate([piece(quad, k) for k in range(4)], axis=1)
                for quad in range(4)
            ],
            axis=0,
        )
        return dot(x, lane_swap[...])

    def part_of(y, quad, k):
        return y[64 * quad : 64 * quad + 64, 128 * k : 128 * k + 128]

    for side, (landed, matrix) in enumerate(((r1l, m_left), (r1r, m_right))):
        settle(landed, sems.at[1 + 28 * side])
        y = swapped(lambda quad, k: flat(landed[:, 4 * quad + k])).astype(BF16)
        for quad in range(4):
            for k in range(4):
                matrix[64 * k : 64 * k + 64, 128 * quad : 128 * quad + 128] = part_of(y, quad, k)

    def columns(which):
        return m_left[:, pl.ds(pl.multiple_of(which * 256, 256), 256)]

    part_out[...] = dot_tn(columns(1 - core), m_right[...]).astype(BF16)
    swap = pltpu.make_async_remote_copy(
        part_out, part_in, sems.at[2], sems.at[3], device_id=beside, device_id_type=MESH
    )
    swap.start()
    part[...] = dot_tn(columns(core), m_right[...])
    swap.wait_recv()
    part[...] = part[...] + part_in[...].astype(F32)
    product = part.reshape(8, 4, 8, 512)

    def lanes(quad):
        return slice(128 * quad, 128 * quad + 128)

    y = swapped(lambda quad, k: product[:, k, :, lanes(quad)].reshape(64, 128).astype(BF16))
    for quad in range(4):
        for k in range(4):
            s2[:, 4 * quad + k] = part_of(y, quad, k).reshape(8, 8, 128).astype(BF16)

    to_cells(s2, r2, 4)
    settle(r2, sems.at[5])

    def to_tile_rows(src, dst):
        for g in range(8):
            x = src(g).astype(F32).reshape(128, 128).astype(BF16)
            y = dot(to_tiles, x)
            for j in range(8):
                dst[j, 16 * g : 16 * g + 16, :] = y[16 * j : 16 * j + 16]

    to_tile_rows(lambda g: r2[16 * g : 16 * g + 16], tri)

    def middle(j, carry):
        that, inverse = normalize(tri[j])
        o = (that * go[...]).astype(BF16)
        onorm[:, tile(j)] = o
        dlin[512:640, tile(j)] = (upper[j] * dot(w_out_t[...], o)).astype(BF16)
        grad = h[j]
        d_t = inverse * (grad - h_mean[j] - that * mean0(grad * that))
        dtri[j] = d_t.astype(BF16)
        return carry

    lax.fori_loop(0, 8, middle, 0, unroll=2)

    for g in range(8):
        s3[16 * g : 16 * g + 16] = to_blocks(dtri, g)
    to_chips(s3, r3, 6)

    def fill(dst, value):
        rows = value.astype(BF16)
        for b in range(2):
            for i in range(64):
                dst[64 * b + i] = rows[2 * i : 2 * i + 2, 128 * b : 128 * b + 128]

    def owner(to_seat, flip):
        return lax.rem(to_seat + flip, 2)

    def scatter(src, dst, flip, k):
        there = dst.at[me]

        def ring(a, first=0):
            to_row = wrap(row + a, 16)
            for b in range(first, 8):
                to_seat = wrap(seat + b, 8)
                start(
                    src.at[to_row * 8 + to_seat], there, sems.at[k], sems.at[k + 1],
                    to_row, 2 * to_seat + owner(to_seat, flip),
                )

        def step(a, carry):
            ring(a)
            return carry

        keep_or_start(
            owner(seat, flip) == core, src.at[chip], there, sems.at[k], sems.at[k + 1], *beside
        )
        lax.fori_loop(6, 16, step, 0)
        lax.fori_loop(1, 6, step, 0)
        ring(0, 1)

    def gather(held, total, dst, flip, k):
        @pl.when(owner(seat, flip) == core)
        def _():
            settle(held, sems.at[k + 1])
            total[...] = jnp.sum(held[...].astype(F32), axis=0).astype(BF16)
            there = dst.at[chip]

            def ring(a, first=0):
                to_row = wrap(row + a, 16)
                for b in range(first, 16):
                    start(
                        total, there, sems.at[k + 2], sems.at[k + 3],
                        to_row, wrap(col + b, 16),
                    )

            def step(a, carry):
                ring(a)
                return carry

            pltpu.make_async_copy(total, there, sems.at[k + 3]).start()
            lax.fori_loop(6, 16, step, 0)
            lax.fori_loop(1, 6, step, 0)
            ring(0, 1)

    def finished(src, held, flip, k):
        settle(src.at[pl.ds(0, 127)], sems.at[k])

        @pl.when(owner(seat, flip) != core)
        def _():
            settle(src.at[0], sems.at[k])

        @pl.when(owner(seat, flip) == core)
        def _():
            settle(held.at[pl.ds(0, 255)], sems.at[k + 2])

    fill(
        g_early,
        jnp.concatenate(
            [dot_nt(onorm[...], dproj[...]), dot_nt(zn[...], dlin[512:640])], axis=1
        ),
    )

    settle(r3, sems.at[7])
    y = swapped(lambda quad, k: flat(r3[:, 4 * quad + k]))
    for quad in range(4):
        for k in range(4):
            dtri_f[:, k, :, lanes(quad)] = part_of(y, quad, k).reshape(8, 8, 128)
    d_own = dtri_f[...].reshape(256, 512).astype(BF16)
    dtri_all[core] = d_own
    swap2 = pltpu.make_async_remote_copy(
        dtri_all.at[core], dtri_all.at[core], sems.at[10], sems.at[11],
        device_id=beside, device_id_type=MESH,
    )
    swap2.start()

    def leave_half(grad, dst, which):
        x = jnp.concatenate(
            [
                jnp.concatenate(
                    [grad[64 * k : 64 * k + 64, lanes(quad)] for k in range(4)], axis=1
                )
                for quad in range(2)
            ],
            axis=0,
        )
        y = dot(x, lane_swap[...])
        for quad in range(2):
            for k in range(4):
                dst[:, 8 * which + 4 * quad + k] = (
                    part_of(y, quad, k).reshape(8, 8, 128).astype(BF16)
                )

    def half_to_cells(src, dst, which, k):
        there = dst.at[chip]
        base = core * 8
        spot = lax.rem(col, 8)

        def ring(a, first=0):
            block = wrap(row8 + a, 8)
            for b in range(first, 8):
                to_col = 8 * which + wrap(spot + b, 8)
                start(
                    src.at[block, to_col], there, sems.at[k], sems.at[k + 1],
                    base + block, to_col,
                )

        def step(a, carry):
            ring(a)
            return carry

        to_col = 8 * which + spot
        keep_or_start(
            jnp.logical_and(mine, to_col == col), src.at[row8, to_col], there,
            sems.at[k], sems.at[k + 1], base + row8, to_col,
        )
        ring(0, 1)
        lax.fori_loop(1, 8, step, 0)

    leave_half(dot_nt(m_right[...], d_own).astype(BF16), s4l, core)
    half_to_cells(s4l, r4l, core, 12)
    swap2.wait_recv()
    leave_half(dot_nt(m_right[...], dtri_all[1 - core]).astype(BF16), s4l, 1 - core)
    half_to_cells(s4l, r4l, 1 - core, 12)
    d_all = dtri_all[...].reshape(512, 512)

    def leave(grad, dst):
        y = swapped(lambda quad, k: grad[64 * k : 64 * k + 64, lanes(quad)])
        for quad in range(4):
            for k in range(4):
                dst[:, 4 * quad + k] = part_of(y, quad, k).reshape(8, 8, 128).astype(BF16)

    leave(dot(m_left[...], d_all).astype(BF16), s4r)
    to_cells(s4r, r4r, 14)
    scatter(g_early, h_early, 1, 16)

    def back(grad, value, slope, base):
        def step(j, carry):
            d = grad[j]
            dlin[base : base + 128, tile(j)] = (d * value[j]).astype(BF16)
            dlin[base + 128 : base + 256, tile(j)] = (d * slope[j]).astype(BF16)
            return carry

        lax.fori_loop(0, 8, step, 0, unroll=2)

    settle(r4l, sems.at[13])
    to_tile_rows(lambda g: r4l[16 * g : 16 * g + 16], grad_l)
    back(grad_l, a_left, b_left, 0)
    fill(g_l, dot_nt(zn[...], dlin[0:256]))
    scatter(g_l, h_l, 0, 20)

    settle(r4r, sems.at[15])
    to_tile_rows(lambda g: r4r[16 * g : 16 * g + 16], grad_r)
    back(grad_r, a_right, b_right, 256)
    fill(g_r, dot_nt(zn[...], dlin[256:512]))
    scatter(g_r, h_r, 1, 24)

    gather(h_early, o_early, a_early, 1, 16)
    gather(h_l, o_l, a_l, 0, 20)

    def finish(j, carry):
        g = dot(w_in[...], dlin[:, tile(j)]) * gi[...]
        normed = zhat[j]
        d = s_z[j] * (g - mean0(g) - normed * mean0(g * normed))
        d = d.T
        for k in range(4):
            d_pair[8 * k + j] = d[32 * k : 32 * k + 32]
        return carry

    lax.fori_loop(0, 4, finish, 0, unroll=2)
    gather(h_r, o_r, a_r, 1, 24)
    lax.fori_loop(4, 8, finish, 0, unroll=2)
    store = pltpu.make_async_copy(d_pair, d_pair_h, local_sems.at[7])
    store.start()

    def collect(dst, lanes, src, base):
        for i in range(64):
            dst[2 * i : 2 * i + 2, lanes] = src[base + i].astype(F32) * scale

    settle(a_early, sems.at[19])
    collect(d_w_out, slice(0, 128), a_early, 0)
    collect(d_w_in, slice(512, 640), a_early, 64)
    weighted = d_w_out[...] * w_out[...].astype(F32)
    d_gain_out[...] = jnp.sum(weighted.T, axis=0, keepdims=True) / gain_out[...]
    settle(a_l, sems.at[23])
    collect(d_w_in, slice(0, 128), a_l, 0)
    collect(d_w_in, slice(128, 256), a_l, 64)
    settle(a_r, sems.at[27])
    collect(d_w_in, slice(256, 384), a_r, 0)
    collect(d_w_in, slice(384, 512), a_r, 64)
    weighted = d_w_in[...] * w_in[...].astype(F32)
    folded = weighted[:, 0:128]
    for b in range(1, 5):
        folded = folded + weighted[:, 128 * b : 128 * b + 128]
    d_gain_in[...] = jnp.sum(folded.T, axis=0, keepdims=True) / gain_in[...]

    store.wait()
    sent(s1l, 0)
    sent(s1r, 28)
    swap.wait_send()
    sent(r2, 4)
    sent(s3, 6)
    swap2.wait_send()
    sent(r4l, 12)
    sent(r4r, 14)
    finished(g_early, h_early, 1, 16)
    finished(g_l, h_l, 0, 20)
    finished(g_r, h_r, 1, 24)


def hand_over(*refs):
    sources, results, held, sems = refs[:5], refs[5:10], refs[10:15], refs[15]
    pieces = []
    for src, dst, buf in zip(sources[1:], results[1:], held[1:]):
        pieces.append((src, dst, buf))
    for n in range(4):
        part = pl.ds(8 * n, 8)
        pieces.append((sources[0].at[part], results[0].at[part], held[0].at[part]))
    loads = []
    stores = []
    for n, (src, dst, buf) in enumerate(pieces):
        loads.append(pltpu.make_async_copy(src, buf, sems.at[n]))
        stores.append(pltpu.make_async_copy(buf, dst, sems.at[8 + n]))
    for load in loads:
        load.start()
    for load, store in zip(loads, stores):
        load.wait()
        store.start()
    for store in stores:
        store.wait()


def body(pair, pair_mask, proj_weight, out_weight, in_gain, out_gain, cotangent):
    vmem = pl.BlockSpec(memory_space=pltpu.VMEM)
    anywhere = pl.BlockSpec(memory_space=pl.ANY)
    V = pltpu.VMEM
    tiles = V((8, 128, 128), F32)
    tiles16 = V((8, 128, 128), BF16)
    by_tile = V((8, 1, 128), F32)
    lanes16 = V((128, 1024), BF16)
    sums = (V((128, 2, 128), BF16), V((256, 2, 128), BF16), V((2, 128), BF16), V((128, 2, 128), BF16))
    scratch = [
        V((128, 8, 128), BF16), V((128, 8, 128), BF16),
        V((8, 16, 8, 128), BF16), V((8, 16, 8, 128), BF16),
        V((8, 16, 8, 128), BF16), V((128, 8, 128), BF16),
        V((128, 8, 128), BF16), V((8, 16, 8, 128), BF16),
        V((8, 16, 8, 128), BF16), V((8, 16, 8, 128), BF16),
        V((128, 8, 128), BF16), V((128, 8, 128), BF16),
        V((512, 512), BF16), by_tile, V((640, 128), BF16), V((128, 128), BF16),
        V((128, 128), F32), V((128, 128), F32),
        tiles, by_tile, lanes16, tiles16, tiles16, tiles, tiles, tiles, tiles,
        lanes16, tiles, tiles, by_tile, V((256, 512), BF16), V((256, 512), BF16),
        V((256, 512), F32), V((256, 512), BF16), V((256, 512), BF16),
        tiles, lanes16, tiles16, V((8, 4, 8, 512), F32), V((2, 256, 512), BF16),
        tiles, tiles, V((640, 1024), BF16),
        *sums, *sums, *sums,
        V(pair.shape, BF16), V(pair_mask.shape, jnp.int32), V((128, 640), BF16), V((128, 128), BF16),
        V((1, 128), F32), V((1, 128), F32), V(pair.shape, BF16), V(pair.shape, F32),
        pltpu.SemaphoreType.DMA((8,)),
        pltpu.SemaphoreType.DMA((30,)),
    ]
    outs = pl.pallas_call(
        kernel,
        out_shape=(
            jax.ShapeDtypeStruct(pair.shape, F32),
            jax.ShapeDtypeStruct((128, 640), F32),
            jax.ShapeDtypeStruct((128, 128), F32),
            jax.ShapeDtypeStruct((1, 128), F32),
            jax.ShapeDtypeStruct((1, 128), F32),
        ),
        in_specs=[anywhere] * 7,
        out_specs=[anywhere] + [vmem] * 4,
        scratch_shapes=scratch,
        name="triangle_back",
        compiler_params=pltpu.CompilerParams(collective_id=0, has_side_effects=True),
    )(
        pair, pair_mask, proj_weight, out_weight,
        in_gain.reshape(1, 128), out_gain.reshape(1, 128), cotangent,
    )
    outs = pl.pallas_call(
        hand_over,
        out_shape=tuple(jax.ShapeDtypeStruct(x.shape, x.dtype) for x in outs),
        in_specs=[anywhere] * 5,
        out_specs=[anywhere] * 5,
        scratch_shapes=[*(V(x.shape, x.dtype) for x in outs), pltpu.SemaphoreType.DMA((16,))],
        name="hand_over",
    )(*outs)
    return (*outs[:3], outs[3].reshape(128), outs[4].reshape(128))


def solution(mesh):
    in_specs = (P("row", "col", None), P("row", "col"), P(), P(), P(), P(), P("row", "col", None))
    out_specs = (P("row", "col", None), P(), P(), P(), P())
    return jax.shard_map(body, mesh=mesh, in_specs=in_specs, out_specs=out_specs, check_vma=False)
```

```python
import jax
import jax.numpy as jnp
from jax import lax
from jax.experimental import pallas as pl
from jax.experimental.pallas import tpu as pltpu
from jax.sharding import PartitionSpec as P

MESH = pl.DeviceIdType.MESH
F32 = jnp.float32
BF16 = jnp.bfloat16
EPS = 1e-05


def settle(ref, sem):
    pltpu.make_async_copy(ref, ref, sem).wait()


def wrap(value, size):
    return jnp.where(value >= size, value - size, value)


def dot(a, b):
    return jnp.dot(a, b, preferred_element_type=F32)


def dot_nt(a, b):
    return lax.dot_general(a, b, (((1,), (1,)), ((), ())), preferred_element_type=F32)


def dot_tn(a, b):
    return lax.dot_general(a, b, (((0,), (0,)), ((), ())), preferred_element_type=F32)


def mean0(x):
    return jnp.sum(x, axis=0, keepdims=True) * (1.0 / x.shape[0])


def normalize(x):
    centred = x - mean0(x)
    inverse = lax.rsqrt(mean0(centred * centred) + EPS)
    return centred * inverse, inverse


def sigmoid(x):
    return 1.0 / (1.0 + jnp.exp(-x))


def start(src, dst, send_sem, recv_sem, row, col):
    pltpu.make_async_remote_copy(
        src, dst, send_sem, recv_sem, device_id=(row, col), device_id_type=MESH
    ).start()


def keep_or_start(mine, src, dst, send_sem, recv_sem, row, col):
    @pl.when(mine)
    def _():
        pltpu.make_async_copy(src, dst, recv_sem).start()

    @pl.when(jnp.logical_not(mine))
    def _():
        start(src, dst, send_sem, recv_sem, row, col)


def kernel(
    pair_h, mask_h, w_in_h, w_out_h, gain_in_h, gain_out_h, cot_h,
    d_pair_h, d_w_in, d_w_out, d_gain_in, d_gain_out,
    s1l, s1r, r1l, r1r, s2a, s2b, r2a, r2b, s3a, s3b, r3a, r3b, s4l, s4r, r4l, r4r,
    lane_swap, cell_mask, w_in_t, w_out_t, gi, go,
    zhat, s_z, zn, left, right, a_left, b_left, a_right, b_right,
    dproj, upper, h, h_mean, m_left, m_right, part, part_out, part_in,
    tri, onorm, dtri, dtri_f, dtri_all, grad_l, grad_r, dlin,
    g_early, h_early, o_early, a_early, g_l, h_l, o_l, a_l, g_r, h_r, o_r, a_r,
    pair, mask, w_in, w_out, gain_in, gain_out, cot, d_pair,
    local_sems, sems,
):
    row = lax.axis_index("row")
    col = lax.axis_index("col")
    me = row * 16 + col
    chip = row * 8 + col // 2
    core = lax.rem(col, 2)
    half = row // 8
    row8 = lax.rem(row, 8)
    cell = row8 * 16 + col
    seat = col // 2
    beside = (row, col + 1 - 2 * core)
    mine = half == core
    scale = 1.0 / 512.0
    loads = [
        pltpu.make_async_copy(src, dst, local_sems.at[n])
        for n, (src, dst) in enumerate(
            (
                (w_in_h, w_in), (w_out_h, w_out), (gain_in_h, gain_in), (gain_out_h, gain_out),
                (mask_h, mask), (pair_h, pair), (cot_h, cot),
            )
        )
    ]
    for load in loads:
        load.start()
    barrier = pltpu.get_barrier_semaphore()

    def hello(a, first=0):
        to_row = wrap(row + a, 16)
        for b in range(first, 16):
            pl.semaphore_signal(
                barrier, inc=1, device_id=(to_row, wrap(col + b, 16)), device_id_type=MESH
            )

    def hello_row(a, carry):
        hello(a)
        return carry

    lax.fori_loop(7, 16, hello_row, 0)
    lax.fori_loop(1, 7, hello_row, 0)
    hello(0, 1)

    def iota(shape, axis):
        return lax.broadcasted_iota(jnp.int32, shape, axis)

    r_i, c_i = iota((128, 128), 0), iota((128, 128), 1)
    to_block = jnp.where(c_i == (r_i & 7) * 16 + (r_i >> 3), 1.0, 0.0).astype(BF16)
    to_tiles = jnp.where(c_i == (r_i & 15) * 8 + (r_i >> 4), 1.0, 0.0).astype(BF16)

    for load in loads[:6]:
        load.wait()
    w_in_t[...] = w_in[...].astype(F32).T.astype(BF16)
    w_out_t[...] = w_out[...].astype(F32).T.astype(BF16)
    gi[...] = jnp.broadcast_to(gain_in[...], (128, 128)).T
    go[...] = jnp.broadcast_to(gain_out[...], (128, 128)).T
    spread = jnp.where(iota((32, 128), 0) == (iota((32, 128), 1) & 31), 1.0, 0.0).astype(BF16)
    wide = dot(mask[...].astype(F32).astype(BF16), spread)
    wide = jnp.where((iota((32, 128), 0) >> 3) == (iota((32, 128), 1) >> 5), wide, 0.0)
    wide = wide[0:8] + wide[8:16] + wide[16:24] + wide[24:32]
    for j in range(8):
        cell_mask[j] = wide[j : j + 1]

    def tile(j):
        return pl.ds(pl.multiple_of(j * 128, 128), 128)

    def cells_in(ref, j):
        rows = jnp.concatenate([ref[8 * k + j] for k in range(4)], axis=0)
        return rows.astype(F32).T

    def project(j, carry):
        normed, inverse = normalize(cells_in(pair, j))
        zhat[j] = normed
        s_z[j] = inverse
        z = (normed * gi[...]).astype(BF16)
        zn[:, tile(j)] = z
        keep = cell_mask[j]
        lin = dot(w_in_t[0:256], z)
        sig = sigmoid(lin[128:256])
        value = keep * sig
        product = value * lin[0:128]
        left[j] = product.astype(BF16)
        a_left[j] = value
        b_left[j] = product * (1.0 - sig)
        lin = dot(w_in_t[256:512], z)
        sig = sigmoid(lin[128:256])
        value = keep * sig
        product = value * lin[0:128]
        right[j] = product.astype(BF16)
        a_right[j] = value
        b_right[j] = product * (1.0 - sig)
        return carry

    lax.fori_loop(0, 8, project, 0, unroll=2)

    def to_blocks(src, g):
        return dot(to_block, src[:, 16 * g : 16 * g + 16, :].reshape(128, 128)).reshape(
            16, 8, 128
        ).astype(BF16)

    for g in range(8):
        s1l[16 * g : 16 * g + 16] = to_blocks(left, g)
        s1r[16 * g : 16 * g + 16] = to_blocks(right, g)

    pl.semaphore_wait(barrier, 255)

    def to_chips(src, dst, k):
        there = dst.at[row8, col]

        def ring(a, first=0):
            to_row = wrap(row + a, 16)
            for b in range(first, 8):
                to_seat = wrap(seat + b, 8)
                start(
                    src.at[to_row * 8 + to_seat], there, sems.at[k], sems.at[k + 1],
                    to_row, 2 * to_seat + half,
                )

        def step(a, carry):
            ring(a)
            return carry

        keep_or_start(mine, src.at[chip], there, sems.at[k], sems.at[k + 1], *beside)
        ring(0, 1)
        lax.fori_loop(1, 16, step, 0)

    def to_cells(src, dst, k):
        there = dst.at[chip]
        base = core * 8

        def ring(a, first=0):
            block = wrap(row8 + a, 8)
            for b in range(first, 16):
                to_col = wrap(col + b, 16)
                start(
                    src.at[block, to_col], there, sems.at[k], sems.at[k + 1],
                    base + block, to_col,
                )

        def step(a, carry):
            ring(a)
            return carry

        keep_or_start(
            mine, src.at[row8, col], there, sems.at[k], sems.at[k + 1], base + row8, col
        )
        ring(0, 1)
        lax.fori_loop(1, 8, step, 0)

    def sent(ref, k):
        settle(ref.at[pl.ds(0, 127)], sems.at[k])

        @pl.when(jnp.logical_not(mine))
        def _():
            settle(ref.at[0], sems.at[k])

    to_chips(s1l, r1l, 0)
    to_chips(s1r, r1r, 28)

    l_i, l_o = iota((512, 512), 0), iota((512, 512), 1)
    lane_swap[...] = jnp.where(
        l_o == ((l_i & 96) << 2) + ((l_i >> 7) << 5) + (l_i & 31), 1.0, 0.0
    ).astype(BF16)

    def gates(j, carry):
        z = zn[:, tile(j)]
        sig = sigmoid(dot(w_in_t[512:640], z))
        c_t = cells_in(cot, j)
        c_sig = c_t * sig
        d_p = c_sig.astype(BF16)
        dproj[:, tile(j)] = d_p
        upper[j] = c_sig * (1.0 - sig)
        grad = dot(w_out[...], d_p) * go[...]
        h[j] = grad
        h_mean[j] = mean0(grad)
        return carry

    loads[6].wait()
    lax.fori_loop(0, 8, gates, 0, unroll=2)

    def flat(x):
        return x.astype(F32).reshape(64, 128).astype(BF16)

    def swapped(piece):
        x = jnp.concatenate(
            [
                jnp.concatenate([piece(quad, k) for k in range(4)], axis=1)
                for quad in range(4)
            ],
            axis=0,
        )
        return dot(x, lane_swap[...])

    def part_of(y, quad, k):
        return y[64 * quad : 64 * quad + 64, 128 * k : 128 * k + 128]

    for side, (landed, matrix) in enumerate(((r1l, m_left), (r1r, m_right))):
        settle(landed, sems.at[1 + 28 * side])
        y = swapped(lambda quad, k: flat(landed[:, 4 * quad + k])).astype(BF16)
        for quad in range(4):
            for k in range(4):
                matrix[64 * k : 64 * k + 64, 128 * quad : 128 * quad + 128] = part_of(y, quad, k)

    def columns(which):
        return m_left[:, pl.ds(pl.multiple_of(which * 256, 256), 256)]

    part_out[...] = dot_tn(columns(1 - core), m_right[...]).astype(BF16)
    swap = pltpu.make_async_remote_copy(
        part_out, part_in, sems.at[2], sems.at[3], device_id=beside, device_id_type=MESH
    )
    swap.start()
    part[...] = dot_tn(columns(core), m_right[...])
    swap.wait_recv()
    part[...] = part[...] + part_in[...].astype(F32)
    product = part.reshape(8, 4, 8, 512)

    def lanes(quad):
        return slice(128 * quad, 128 * quad + 128)

    y = swapped(lambda quad, k: product[:, k, :, lanes(quad)].reshape(64, 128).astype(BF16))
    for quad in range(4):
        for k in range(4):
            block = part_of(y, quad, k).reshape(8, 8, 128)
            s2a[:, 4 * quad + k] = block[:, 0:4].astype(BF16)
            s2b[:, 4 * quad + k] = block[:, 4:8].astype(BF16)

    to_cells(s2a, r2a, 4)
    to_cells(s2b, r2b, 30)

    def to_tile_rows(src, dst):
        for g in range(8):
            x = src(g).astype(F32).reshape(128, 128).astype(BF16)
            y = dot(to_tiles, x)
            for j in range(8):
                dst[j, 16 * g : 16 * g + 16, :] = y[16 * j : 16 * j + 16]


    def middle(j, carry):
        that, inverse = normalize(tri[j])
        o = (that * go[...]).astype(BF16)
        onorm[:, tile(j)] = o
        dlin[512:640, tile(j)] = (upper[j] * dot(w_out_t[...], o)).astype(BF16)
        grad = h[j]
        d_t = inverse * (grad - h_mean[j] - that * mean0(grad * that))
        dtri[j] = d_t.astype(BF16)
        return carry

    to_half_block = jnp.where(c_i == (r_i & 3) * 32 + (r_i >> 2), 1.0, 0.0).astype(BF16)
    to_half_tiles = jnp.where(c_i == (r_i & 31) * 4 + (r_i >> 5), 1.0, 0.0).astype(BF16)

    def middle_half(landed, leaving, landed_sem, first):
        settle(landed, sems.at[landed_sem])
        for g in range(4):
            channels = slice(32 * g, 32 * g + 32)
            y = dot(to_half_tiles, landed[channels].astype(F32).reshape(128, 128).astype(BF16))
            for j in range(4):
                tri[first + j, channels, :] = y[32 * j : 32 * j + 32]
        lax.fori_loop(first, first + 4, middle, 0, unroll=2)
        for g in range(4):
            channels = slice(32 * g, 32 * g + 32)
            y = dot(to_half_block, dtri[first : first + 4, channels, :].reshape(128, 128))
            leaving[channels] = y.reshape(32, 4, 128).astype(BF16)

    middle_half(r2a, s3a, 5, 0)
    to_chips(s3a, r3a, 6)
    middle_half(r2b, s3b, 31, 4)
    to_chips(s3b, r3b, 32)

    def fill(dst, value):
        rows = value.astype(BF16)
        for b in range(2):
            for i in range(64):
                dst[64 * b + i] = rows[2 * i : 2 * i + 2, 128 * b : 128 * b + 128]

    def owner(to_seat, flip):
        return lax.rem(to_seat + flip, 2)

    def scatter(src, dst, flip, k):
        there = dst.at[me]

        def ring(a, first=0):
            to_row = wrap(row + a, 16)
            for b in range(first, 8):
                to_seat = wrap(seat + b, 8)
                start(
                    src.at[to_row * 8 + to_seat], there, sems.at[k], sems.at[k + 1],
                    to_row, 2 * to_seat + owner(to_seat, flip),
                )

        def step(a, carry):
            ring(a)
            return carry

        keep_or_start(
            owner(seat, flip) == core, src.at[chip], there, sems.at[k], sems.at[k + 1], *beside
        )
        lax.fori_loop(6, 16, step, 0)
        lax.fori_loop(1, 6, step, 0)
        ring(0, 1)

    def gather(held, total, dst, flip, k):
        @pl.when(owner(seat, flip) == core)
        def _():
            settle(held, sems.at[k + 1])
            total[...] = jnp.sum(held[...].astype(F32), axis=0).astype(BF16)
            there = dst.at[chip]

            def ring(a, first=0):
                to_row = wrap(row + a, 16)
                for b in range(first, 16):
                    start(
                        total, there, sems.at[k + 2], sems.at[k + 3],
                        to_row, wrap(col + b, 16),
                    )

            def step(a, carry):
                ring(a)
                return carry

            pltpu.make_async_copy(total, there, sems.at[k + 3]).start()
            lax.fori_loop(6, 16, step, 0)
            lax.fori_loop(1, 6, step, 0)
            ring(0, 1)

    def finished(src, held, flip, k):
        settle(src.at[pl.ds(0, 127)], sems.at[k])

        @pl.when(owner(seat, flip) != core)
        def _():
            settle(src.at[0], sems.at[k])

        @pl.when(owner(seat, flip) == core)
        def _():
            settle(held.at[pl.ds(0, 255)], sems.at[k + 2])

    fill(
        g_early,
        jnp.concatenate(
            [dot_nt(onorm[...], dproj[...]), dot_nt(zn[...], dlin[512:640])], axis=1
        ),
    )

    settle(r3a, sems.at[7])
    settle(r3b, sems.at[33])

    def joined(q):
        both = jnp.concatenate([r3a[:, q].astype(F32), r3b[:, q].astype(F32)], axis=1)
        return both.reshape(64, 128).astype(BF16)

    y = swapped(lambda quad, k: joined(4 * quad + k))
    for quad in range(4):
        for k in range(4):
            dtri_f[:, k, :, lanes(quad)] = part_of(y, quad, k).reshape(8, 8, 128)
    d_own = dtri_f[...].reshape(256, 512).astype(BF16)
    dtri_all[core] = d_own
    swap2 = pltpu.make_async_remote_copy(
        dtri_all.at[core], dtri_all.at[core], sems.at[10], sems.at[11],
        device_id=beside, device_id_type=MESH,
    )
    swap2.start()

    def leave_half(grad, dst, which):
        x = jnp.concatenate(
            [
                jnp.concatenate(
                    [grad[64 * k : 64 * k + 64, lanes(quad)] for k in range(4)], axis=1
                )
                for quad in range(2)
            ],
            axis=0,
        )
        y = dot(x, lane_swap[...])
        for quad in range(2):
            for k in range(4):
                dst[:, 8 * which + 4 * quad + k] = (
                    part_of(y, quad, k).reshape(8, 8, 128).astype(BF16)
                )

    def half_to_cells(src, dst, which, k):
        there = dst.at[chip]
        base = core * 8
        spot = lax.rem(col, 8)

        def ring(a, first=0):
            block = wrap(row8 + a, 8)
            for b in range(first, 8):
                to_col = 8 * which + wrap(spot + b, 8)
                start(
                    src.at[block, to_col], there, sems.at[k], sems.at[k + 1],
                    base + block, to_col,
                )

        def step(a, carry):
            ring(a)
            return carry

        to_col = 8 * which + spot
        keep_or_start(
            jnp.logical_and(mine, to_col == col), src.at[row8, to_col], there,
            sems.at[k], sems.at[k + 1], base + row8, to_col,
        )
        ring(0, 1)
        lax.fori_loop(1, 8, step, 0)

    leave_half(dot_nt(m_right[...], d_own).astype(BF16), s4l, core)
    half_to_cells(s4l, r4l, core, 12)
    swap2.wait_recv()
    leave_half(dot_nt(m_right[...], dtri_all[1 - core]).astype(BF16), s4l, 1 - core)
    half_to_cells(s4l, r4l, 1 - core, 12)
    d_all = dtri_all[...].reshape(512, 512)

    def leave(grad, dst):
        y = swapped(lambda quad, k: grad[64 * k : 64 * k + 64, lanes(quad)])
        for quad in range(4):
            for k in range(4):
                dst[:, 4 * quad + k] = part_of(y, quad, k).reshape(8, 8, 128).astype(BF16)

    leave(dot(m_left[...], d_all).astype(BF16), s4r)
    to_cells(s4r, r4r, 14)
    scatter(g_early, h_early, 1, 16)

    def back(grad, value, slope, base):
        def step(j, carry):
            d = grad[j]
            dlin[base : base + 128, tile(j)] = (d * value[j]).astype(BF16)
            dlin[base + 128 : base + 256, tile(j)] = (d * slope[j]).astype(BF16)
            return carry

        lax.fori_loop(0, 8, step, 0, unroll=2)

    settle(r4l, sems.at[13])
    to_tile_rows(lambda g: r4l[16 * g : 16 * g + 16], grad_l)
    back(grad_l, a_left, b_left, 0)
    fill(g_l, dot_nt(zn[...], dlin[0:256]))
    scatter(g_l, h_l, 0, 20)

    settle(r4r, sems.at[15])
    to_tile_rows(lambda g: r4r[16 * g : 16 * g + 16], grad_r)
    back(grad_r, a_right, b_right, 256)
    fill(g_r, dot_nt(zn[...], dlin[256:512]))
    scatter(g_r, h_r, 1, 24)

    gather(h_early, o_early, a_early, 1, 16)
    gather(h_l, o_l, a_l, 0, 20)

    def finish(j, carry):
        g = dot(w_in[...], dlin[:, tile(j)]) * gi[...]
        normed = zhat[j]
        d = s_z[j] * (g - mean0(g) - normed * mean0(g * normed))
        d = d.T
        for k in range(4):
            d_pair[8 * k + j] = d[32 * k : 32 * k + 32]
        return carry

    lax.fori_loop(0, 4, finish, 0, unroll=2)
    gather(h_r, o_r, a_r, 1, 24)
    lax.fori_loop(4, 8, finish, 0, unroll=2)
    store = pltpu.make_async_copy(d_pair, d_pair_h, local_sems.at[7])
    store.start()

    def collect(dst, lanes, src, base):
        for i in range(64):
            dst[2 * i : 2 * i + 2, lanes] = src[base + i].astype(F32) * scale

    settle(a_early, sems.at[19])
    collect(d_w_out, slice(0, 128), a_early, 0)
    collect(d_w_in, slice(512, 640), a_early, 64)
    weighted = d_w_out[...] * w_out[...].astype(F32)
    d_gain_out[...] = jnp.sum(weighted.T, axis=0, keepdims=True) / gain_out[...]
    settle(a_l, sems.at[23])
    collect(d_w_in, slice(0, 128), a_l, 0)
    collect(d_w_in, slice(128, 256), a_l, 64)
    settle(a_r, sems.at[27])
    collect(d_w_in, slice(256, 384), a_r, 0)
    collect(d_w_in, slice(384, 512), a_r, 64)
    weighted = d_w_in[...] * w_in[...].astype(F32)
    folded = weighted[:, 0:128]
    for b in range(1, 5):
        folded = folded + weighted[:, 128 * b : 128 * b + 128]
    d_gain_in[...] = jnp.sum(folded.T, axis=0, keepdims=True) / gain_in[...]

    store.wait()
    sent(s1l, 0)
    sent(s1r, 28)
    swap.wait_send()
    sent(r2a, 4)
    sent(r2b, 30)
    sent(s3a, 6)
    sent(s3b, 32)
    swap2.wait_send()
    sent(r4l, 12)
    sent(r4r, 14)
    finished(g_early, h_early, 1, 16)
    finished(g_l, h_l, 0, 20)
    finished(g_r, h_r, 1, 24)


def hand_over(*refs):
    sources, results, held, sems = refs[:5], refs[5:10], refs[10:15], refs[15]
    pieces = []
    for src, dst, buf in zip(sources[1:], results[1:], held[1:]):
        pieces.append((src, dst, buf))
    for n in range(4):
        part = pl.ds(8 * n, 8)
        pieces.append((sources[0].at[part], results[0].at[part], held[0].at[part]))
    loads = []
    stores = []
    for n, (src, dst, buf) in enumerate(pieces):
        loads.append(pltpu.make_async_copy(src, buf, sems.at[n]))
        stores.append(pltpu.make_async_copy(buf, dst, sems.at[8 + n]))
    for load in loads:
        load.start()
    for load, store in zip(loads, stores):
        load.wait()
        store.start()
    for store in stores:
        store.wait()


def body(pair, pair_mask, proj_weight, out_weight, in_gain, out_gain, cotangent):
    vmem = pl.BlockSpec(memory_space=pltpu.VMEM)
    anywhere = pl.BlockSpec(memory_space=pl.ANY)
    V = pltpu.VMEM
    tiles = V((8, 128, 128), F32)
    tiles16 = V((8, 128, 128), BF16)
    by_tile = V((8, 1, 128), F32)
    lanes16 = V((128, 1024), BF16)
    sums = (V((128, 2, 128), BF16), V((256, 2, 128), BF16), V((2, 128), BF16), V((128, 2, 128), BF16))
    scratch = [
        V((128, 8, 128), BF16), V((128, 8, 128), BF16),
        V((8, 16, 8, 128), BF16), V((8, 16, 8, 128), BF16),
        V((8, 16, 4, 128), BF16), V((8, 16, 4, 128), BF16),
        V((128, 4, 128), BF16), V((128, 4, 128), BF16),
        V((128, 4, 128), BF16), V((128, 4, 128), BF16),
        V((8, 16, 4, 128), BF16), V((8, 16, 4, 128), BF16),
        V((8, 16, 8, 128), BF16), V((8, 16, 8, 128), BF16),
        V((128, 8, 128), BF16), V((128, 8, 128), BF16),
        V((512, 512), BF16), by_tile, V((640, 128), BF16), V((128, 128), BF16),
        V((128, 128), F32), V((128, 128), F32),
        tiles, by_tile, lanes16, tiles16, tiles16, tiles, tiles, tiles, tiles,
        lanes16, tiles, tiles, by_tile, V((256, 512), BF16), V((256, 512), BF16),
        V((256, 512), F32), V((256, 512), BF16), V((256, 512), BF16),
        tiles, lanes16, tiles16, V((8, 4, 8, 512), F32), V((2, 256, 512), BF16),
        tiles, tiles, V((640, 1024), BF16),
        *sums, *sums, *sums,
        V(pair.shape, BF16), V(pair_mask.shape, jnp.int32), V((128, 640), BF16), V((128, 128), BF16),
        V((1, 128), F32), V((1, 128), F32), V(pair.shape, BF16), V(pair.shape, F32),
        pltpu.SemaphoreType.DMA((8,)),
        pltpu.SemaphoreType.DMA((34,)),
    ]
    outs = pl.pallas_call(
        kernel,
        out_shape=(
            jax.ShapeDtypeStruct(pair.shape, F32),
            jax.ShapeDtypeStruct((128, 640), F32),
            jax.ShapeDtypeStruct((128, 128), F32),
            jax.ShapeDtypeStruct((1, 128), F32),
            jax.ShapeDtypeStruct((1, 128), F32),
        ),
        in_specs=[anywhere] * 7,
        out_specs=[anywhere] + [vmem] * 4,
        scratch_shapes=scratch,
        name="triangle_back",
        compiler_params=pltpu.CompilerParams(collective_id=0, has_side_effects=True),
    )(
        pair, pair_mask, proj_weight, out_weight,
        in_gain.reshape(1, 128), out_gain.reshape(1, 128), cotangent,
    )
    outs = pl.pallas_call(
        hand_over,
        out_shape=tuple(jax.ShapeDtypeStruct(x.shape, x.dtype) for x in outs),
        in_specs=[anywhere] * 5,
        out_specs=[anywhere] * 5,
        scratch_shapes=[*(V(x.shape, x.dtype) for x in outs), pltpu.SemaphoreType.DMA((16,))],
        name="hand_over",
    )(*outs)
    return (*outs[:3], outs[3].reshape(128), outs[4].reshape(128))


def solution(mesh):
    in_specs = (P("row", "col", None), P("row", "col"), P(), P(), P(), P(), P("row", "col", None))
    out_specs = (P("row", "col", None), P(), P(), P(), P())
    return jax.shard_map(body, mesh=mesh, in_specs=in_specs, out_specs=out_specs, check_vma=False)
```

```python
import jax
import jax.numpy as jnp
from jax import lax
from jax.experimental import pallas as pl
from jax.experimental.pallas import tpu as pltpu
from jax.sharding import PartitionSpec as P

MESH = pl.DeviceIdType.MESH
F32 = jnp.float32
BF16 = jnp.bfloat16
EPS = 1e-05


def settle(ref, sem):
    pltpu.make_async_copy(ref, ref, sem).wait()


def wrap(value, size):
    return jnp.where(value >= size, value - size, value)


def dot(a, b):
    return jnp.dot(a, b, preferred_element_type=F32)


def dot_nt(a, b):
    return lax.dot_general(a, b, (((1,), (1,)), ((), ())), preferred_element_type=F32)


def dot_tn(a, b):
    return lax.dot_general(a, b, (((0,), (0,)), ((), ())), preferred_element_type=F32)


def mean0(x):
    return jnp.sum(x, axis=0, keepdims=True) * (1.0 / x.shape[0])


def normalize(x):
    centred = x - mean0(x)
    inverse = lax.rsqrt(mean0(centred * centred) + EPS)
    return centred * inverse, inverse


def sigmoid(x):
    return 1.0 / (1.0 + jnp.exp(-x))


def start(src, dst, send_sem, recv_sem, row, col):
    pltpu.make_async_remote_copy(
        src, dst, send_sem, recv_sem, device_id=(row, col), device_id_type=MESH
    ).start()


def keep_or_start(mine, src, dst, send_sem, recv_sem, row, col):
    @pl.when(mine)
    def _():
        pltpu.make_async_copy(src, dst, recv_sem).start()

    @pl.when(jnp.logical_not(mine))
    def _():
        start(src, dst, send_sem, recv_sem, row, col)


def kernel(
    pair_h, mask_h, w_in_h, w_out_h, gain_in_h, gain_out_h, cot_h,
    d_pair_h, d_w_in, d_w_out, d_gain_in, d_gain_out,
    s1l, s1r, r1l, r1r, s2a, s2b, r2a, r2b, s3a, s3b, r3a, r3b, s4l, s4r, r4l, r4r,
    lane_swap, cell_mask, w_in_t, w_out_t, gi, go,
    zhat, s_z, zn, left, right, a_left, b_left, a_right, b_right,
    dproj, upper, h, h_mean, m_left, m_right, part, part_out, part_in,
    tri, onorm, dtri, dtri_f, dtri_all, grad_l, grad_r, dlin,
    g_early, h_early, o_early, a_early, g_l, h_l, o_l, a_l, g_r, h_r, o_r, a_r,
    pair, mask, w_in, w_out, gain_in, gain_out, cot, d_pair,
    local_sems, sems,
):
    row = lax.axis_index("row")
    col = lax.axis_index("col")
    me = row * 16 + col
    chip = row * 8 + col // 2
    core = lax.rem(col, 2)
    half = row // 8
    row8 = lax.rem(row, 8)
    cell = row8 * 16 + col
    seat = col // 2
    beside = (row, col + 1 - 2 * core)
    mine = half == core
    scale = 1.0 / 512.0
    loads = [
        pltpu.make_async_copy(src, dst, local_sems.at[n])
        for n, (src, dst) in enumerate(
            (
                (w_in_h, w_in), (w_out_h, w_out), (gain_in_h, gain_in), (gain_out_h, gain_out),
                (mask_h, mask), (pair_h, pair), (cot_h, cot),
            )
        )
    ]
    for load in loads:
        load.start()
    barrier = pltpu.get_barrier_semaphore()

    def hello(a, first=0):
        to_row = wrap(row + a, 16)
        for b in range(first, 16):
            pl.semaphore_signal(
                barrier, inc=1, device_id=(to_row, wrap(col + b, 16)), device_id_type=MESH
            )

    def hello_row(a, carry):
        hello(a)
        return carry

    lax.fori_loop(7, 16, hello_row, 0)
    lax.fori_loop(1, 7, hello_row, 0)
    hello(0, 1)

    def iota(shape, axis):
        return lax.broadcasted_iota(jnp.int32, shape, axis)

    r_i, c_i = iota((128, 128), 0), iota((128, 128), 1)
    to_block = jnp.where(c_i == (r_i & 7) * 16 + (r_i >> 3), 1.0, 0.0).astype(BF16)
    to_tiles = jnp.where(c_i == (r_i & 15) * 8 + (r_i >> 4), 1.0, 0.0).astype(BF16)

    for load in loads[:6]:
        load.wait()
    w_in_t[...] = w_in[...].astype(F32).T.astype(BF16)
    w_out_t[...] = w_out[...].astype(F32).T.astype(BF16)
    gi[...] = jnp.broadcast_to(gain_in[...], (128, 128)).T
    go[...] = jnp.broadcast_to(gain_out[...], (128, 128)).T
    spread = jnp.where(iota((32, 128), 0) == (iota((32, 128), 1) & 31), 1.0, 0.0).astype(BF16)
    wide = dot(mask[...].astype(F32).astype(BF16), spread)
    wide = jnp.where((iota((32, 128), 0) >> 3) == (iota((32, 128), 1) >> 5), wide, 0.0)
    wide = wide[0:8] + wide[8:16] + wide[16:24] + wide[24:32]
    for j in range(8):
        cell_mask[j] = wide[j : j + 1]

    def tile(j):
        return pl.ds(pl.multiple_of(j * 128, 128), 128)

    def cells_in(ref, j):
        rows = jnp.concatenate([ref[8 * k + j] for k in range(4)], axis=0)
        return rows.astype(F32).T

    def project(j, carry):
        normed, inverse = normalize(cells_in(pair, j))
        zhat[j] = normed
        s_z[j] = inverse
        z = (normed * gi[...]).astype(BF16)
        zn[:, tile(j)] = z
        keep = cell_mask[j]
        lin = dot(w_in_t[0:256], z)
        sig = sigmoid(lin[128:256])
        value = keep * sig
        product = value * lin[0:128]
        left[j] = product.astype(BF16)
        a_left[j] = value
        b_left[j] = product * (1.0 - sig)
        lin = dot(w_in_t[256:512], z)
        sig = sigmoid(lin[128:256])
        value = keep * sig
        product = value * lin[0:128]
        right[j] = product.astype(BF16)
        a_right[j] = value
        b_right[j] = product * (1.0 - sig)
        return carry

    lax.fori_loop(0, 8, project, 0, unroll=2)

    def to_blocks(src, g):
        return dot(to_block, src[:, 16 * g : 16 * g + 16, :].reshape(128, 128)).reshape(
            16, 8, 128
        ).astype(BF16)

    for g in range(8):
        s1l[16 * g : 16 * g + 16] = to_blocks(left, g)
        s1r[16 * g : 16 * g + 16] = to_blocks(right, g)

    pl.semaphore_wait(barrier, 255)

    def to_chips(src, dst, k):
        there = dst.at[row8, col]

        def ring(a, first=0):
            to_row = wrap(row + a, 16)
            for b in range(first, 8):
                to_seat = wrap(seat + b, 8)
                start(
                    src.at[to_row * 8 + to_seat], there, sems.at[k], sems.at[k + 1],
                    to_row, 2 * to_seat + half,
                )

        def step(a, carry):
            ring(a)
            return carry

        keep_or_start(mine, src.at[chip], there, sems.at[k], sems.at[k + 1], *beside)
        ring(0, 1)
        lax.fori_loop(1, 16, step, 0)

    def to_cells(src, dst, k):
        there = dst.at[chip]
        base = core * 8

        def ring(a, first=0):
            block = wrap(row8 + a, 8)
            for b in range(first, 16):
                to_col = wrap(col + b, 16)
                start(
                    src.at[block, to_col], there, sems.at[k], sems.at[k + 1],
                    base + block, to_col,
                )

        def step(a, carry):
            ring(a)
            return carry

        keep_or_start(
            mine, src.at[row8, col], there, sems.at[k], sems.at[k + 1], base + row8, col
        )
        ring(0, 1)
        lax.fori_loop(1, 8, step, 0)

    def sent(ref, k):
        settle(ref.at[pl.ds(0, 127)], sems.at[k])

        @pl.when(jnp.logical_not(mine))
        def _():
            settle(ref.at[0], sems.at[k])

    to_chips(s1l, r1l, 0)
    to_chips(s1r, r1r, 28)

    l_i, l_o = iota((512, 512), 0), iota((512, 512), 1)
    lane_swap[...] = jnp.where(
        l_o == ((l_i & 96) << 2) + ((l_i >> 7) << 5) + (l_i & 31), 1.0, 0.0
    ).astype(BF16)

    def gates(j, carry):
        z = zn[:, tile(j)]
        sig = sigmoid(dot(w_in_t[512:640], z))
        c_t = cells_in(cot, j)
        c_sig = c_t * sig
        d_p = c_sig.astype(BF16)
        dproj[:, tile(j)] = d_p
        upper[j] = c_sig * (1.0 - sig)
        grad = dot(w_out[...], d_p) * go[...]
        h[j] = grad
        h_mean[j] = mean0(grad)
        return carry

    loads[6].wait()
    lax.fori_loop(0, 8, gates, 0, unroll=2)

    def flat(x):
        return x.astype(F32).reshape(64, 128).astype(BF16)

    def swapped(piece):
        x = jnp.concatenate(
            [
                jnp.concatenate([piece(quad, k) for k in range(4)], axis=1)
                for quad in range(4)
            ],
            axis=0,
        )
        return dot(x, lane_swap[...])

    def part_of(y, quad, k):
        return y[64 * quad : 64 * quad + 64, 128 * k : 128 * k + 128]

    for side, (landed, matrix) in enumerate(((r1l, m_left), (r1r, m_right))):
        settle(landed, sems.at[1 + 28 * side])
        y = swapped(lambda quad, k: flat(landed[:, 4 * quad + k])).astype(BF16)
        for quad in range(4):
            for k in range(4):
                matrix[64 * k : 64 * k + 64, 128 * quad : 128 * quad + 128] = part_of(y, quad, k)

    def columns(which):
        return m_left[:, pl.ds(pl.multiple_of(which * 256, 256), 256)]

    part_out[...] = dot_tn(columns(1 - core), m_right[...]).astype(BF16)
    swap = pltpu.make_async_remote_copy(
        part_out, part_in, sems.at[2], sems.at[3], device_id=beside, device_id_type=MESH
    )
    swap.start()
    part[...] = dot_tn(columns(core), m_right[...])
    swap.wait_recv()
    part[...] = part[...] + part_in[...].astype(F32)
    product = part.reshape(8, 4, 8, 512)

    def lanes(quad):
        return slice(128 * quad, 128 * quad + 128)

    y = swapped(lambda quad, k: product[:, k, :, lanes(quad)].reshape(64, 128).astype(BF16))
    for quad in range(4):
        for k in range(4):
            block = part_of(y, quad, k).reshape(8, 8, 128)
            s2a[:, 4 * quad + k] = block[:, 0:4].astype(BF16)
            s2b[:, 4 * quad + k] = block[:, 4:8].astype(BF16)

    to_cells(s2a, r2a, 4)
    to_cells(s2b, r2b, 30)

    def to_tile_rows(src, dst):
        for g in range(8):
            x = src(g).astype(F32).reshape(128, 128).astype(BF16)
            y = dot(to_tiles, x)
            for j in range(8):
                dst[j, 16 * g : 16 * g + 16, :] = y[16 * j : 16 * j + 16]


    def middle(j, carry):
        that, inverse = normalize(tri[j])
        o = (that * go[...]).astype(BF16)
        onorm[:, tile(j)] = o
        dlin[512:640, tile(j)] = (upper[j] * dot(w_out_t[...], o)).astype(BF16)
        grad = h[j]
        d_t = inverse * (grad - h_mean[j] - that * mean0(grad * that))
        dtri[j] = d_t.astype(BF16)
        return carry

    to_half_block = jnp.where(c_i == (r_i & 3) * 32 + (r_i >> 2), 1.0, 0.0).astype(BF16)
    to_half_tiles = jnp.where(c_i == (r_i & 31) * 4 + (r_i >> 5), 1.0, 0.0).astype(BF16)

    def middle_half(landed, leaving, landed_sem, first):
        settle(landed, sems.at[landed_sem])
        for g in range(4):
            channels = slice(32 * g, 32 * g + 32)
            y = dot(to_half_tiles, landed[channels].astype(F32).reshape(128, 128).astype(BF16))
            for j in range(4):
                tri[first + j, channels, :] = y[32 * j : 32 * j + 32]
        lax.fori_loop(first, first + 4, middle, 0, unroll=2)
        for g in range(4):
            channels = slice(32 * g, 32 * g + 32)
            y = dot(to_half_block, dtri[first : first + 4, channels, :].reshape(128, 128))
            leaving[channels] = y.reshape(32, 4, 128).astype(BF16)

    middle_half(r2a, s3a, 5, 0)
    to_chips(s3a, r3a, 6)
    middle_half(r2b, s3b, 31, 4)
    to_chips(s3b, r3b, 32)

    def fill(dst, value):
        rows = value.astype(BF16)
        for b in range(2):
            for i in range(64):
                dst[64 * b + i] = rows[2 * i : 2 * i + 2, 128 * b : 128 * b + 128]

    def owner(to_seat, flip):
        return lax.rem(to_seat + flip, 2)

    def scatter(src, dst, flip, k):
        there = dst.at[me]

        def ring(a, first=0):
            to_row = wrap(row + a, 16)
            for b in range(first, 8):
                to_seat = wrap(seat + b, 8)
                start(
                    src.at[to_row * 8 + to_seat], there, sems.at[k], sems.at[k + 1],
                    to_row, 2 * to_seat + owner(to_seat, flip),
                )

        def step(a, carry):
            ring(a)
            return carry

        keep_or_start(
            owner(seat, flip) == core, src.at[chip], there, sems.at[k], sems.at[k + 1], *beside
        )
        lax.fori_loop(6, 16, step, 0)
        lax.fori_loop(1, 6, step, 0)
        ring(0, 1)

    def gather(held, total, dst, flip, k):
        @pl.when(owner(seat, flip) == core)
        def _():
            settle(held, sems.at[k + 1])
            total[...] = jnp.sum(held[...].astype(F32), axis=0).astype(BF16)
            there = dst.at[chip]

            def ring(a, first=0):
                to_row = wrap(row + a, 16)
                for b in range(first, 16):
                    start(
                        total, there, sems.at[k + 2], sems.at[k + 3],
                        to_row, wrap(col + b, 16),
                    )

            def step(a, carry):
                ring(a)
                return carry

            pltpu.make_async_copy(total, there, sems.at[k + 3]).start()
            lax.fori_loop(6, 16, step, 0)
            lax.fori_loop(1, 6, step, 0)
            ring(0, 1)

    def finished(src, held, flip, k):
        settle(src.at[pl.ds(0, 127)], sems.at[k])

        @pl.when(owner(seat, flip) != core)
        def _():
            settle(src.at[0], sems.at[k])

        @pl.when(owner(seat, flip) == core)
        def _():
            settle(held.at[pl.ds(0, 255)], sems.at[k + 2])

    fill(
        g_early,
        jnp.concatenate(
            [dot_nt(onorm[...], dproj[...]), dot_nt(zn[...], dlin[512:640])], axis=1
        ),
    )

    settle(r3a, sems.at[7])
    settle(r3b, sems.at[33])

    def joined(q):
        both = jnp.concatenate([r3a[:, q].astype(F32), r3b[:, q].astype(F32)], axis=1)
        return both.reshape(64, 128).astype(BF16)

    y = swapped(lambda quad, k: joined(4 * quad + k))
    for quad in range(4):
        for k in range(4):
            dtri_f[:, k, :, lanes(quad)] = part_of(y, quad, k).reshape(8, 8, 128)
    d_own = dtri_f[...].reshape(256, 512).astype(BF16)
    dtri_all[core] = d_own
    swap2 = pltpu.make_async_remote_copy(
        dtri_all.at[core], dtri_all.at[core], sems.at[10], sems.at[11],
        device_id=beside, device_id_type=MESH,
    )
    swap2.start()

    def leave_half(grad, dst, which):
        x = jnp.concatenate(
            [
                jnp.concatenate(
                    [grad[64 * k : 64 * k + 64, lanes(quad)] for k in range(4)], axis=1
                )
                for quad in range(2)
            ],
            axis=0,
        )
        y = dot(x, lane_swap[...])
        for quad in range(2):
            for k in range(4):
                dst[:, 8 * which + 4 * quad + k] = (
                    part_of(y, quad, k).reshape(8, 8, 128).astype(BF16)
                )

    def half_to_cells(src, dst, which, k):
        there = dst.at[chip]
        base = core * 8
        spot = lax.rem(col, 8)

        def ring(a, first=0):
            block = wrap(row8 + a, 8)
            for b in range(first, 8):
                to_col = 8 * which + wrap(spot + b, 8)
                start(
                    src.at[block, to_col], there, sems.at[k], sems.at[k + 1],
                    base + block, to_col,
                )

        def step(a, carry):
            ring(a)
            return carry

        to_col = 8 * which + spot
        keep_or_start(
            jnp.logical_and(mine, to_col == col), src.at[row8, to_col], there,
            sems.at[k], sems.at[k + 1], base + row8, to_col,
        )
        ring(0, 1)
        lax.fori_loop(1, 8, step, 0)

    leave_half(dot_nt(m_right[...], d_own).astype(BF16), s4l, core)
    half_to_cells(s4l, r4l, core, 12)
    swap2.wait_recv()
    leave_half(dot_nt(m_right[...], dtri_all[1 - core]).astype(BF16), s4l, 1 - core)
    half_to_cells(s4l, r4l, 1 - core, 12)
    d_all = dtri_all[...].reshape(512, 512)

    def leave(grad, dst):
        y = swapped(lambda quad, k: grad[64 * k : 64 * k + 64, lanes(quad)])
        for quad in range(4):
            for k in range(4):
                dst[:, 4 * quad + k] = part_of(y, quad, k).reshape(8, 8, 128).astype(BF16)

    leave(dot(m_left[...], d_all).astype(BF16), s4r)
    to_cells(s4r, r4r, 14)
    scatter(g_early, h_early, 1, 16)

    def back(grad, value, slope, base):
        def step(j, carry):
            d = grad[j]
            dlin[base : base + 128, tile(j)] = (d * value[j]).astype(BF16)
            dlin[base + 128 : base + 256, tile(j)] = (d * slope[j]).astype(BF16)
            return carry

        lax.fori_loop(0, 8, step, 0, unroll=2)

    settle(r4l, sems.at[13])
    to_tile_rows(lambda g: r4l[16 * g : 16 * g + 16], grad_l)
    back(grad_l, a_left, b_left, 0)
    fill(g_l, dot_nt(zn[...], dlin[0:256]))
    scatter(g_l, h_l, 0, 20)

    settle(r4r, sems.at[15])
    to_tile_rows(lambda g: r4r[16 * g : 16 * g + 16], grad_r)
    back(grad_r, a_right, b_right, 256)
    fill(g_r, dot_nt(zn[...], dlin[256:512]))
    scatter(g_r, h_r, 1, 24)

    gather(h_early, o_early, a_early, 1, 16)
    gather(h_l, o_l, a_l, 0, 20)

    def finish(j, carry):
        g = dot(w_in[...], dlin[:, tile(j)]) * gi[...]
        normed = zhat[j]
        d = s_z[j] * (g - mean0(g) - normed * mean0(g * normed))
        d = d.T
        for k in range(4):
            d_pair[8 * k + j] = d[32 * k : 32 * k + 32]
        return carry

    lax.fori_loop(0, 4, finish, 0, unroll=2)
    gather(h_r, o_r, a_r, 1, 24)
    lax.fori_loop(4, 8, finish, 0, unroll=2)
    store = pltpu.make_async_copy(d_pair, d_pair_h, local_sems.at[7])
    store.start()

    def collect(dst, lanes, src, base):
        for i in range(64):
            dst[2 * i : 2 * i + 2, lanes] = src[base + i].astype(F32) * scale

    settle(a_early, sems.at[19])
    collect(d_w_out, slice(0, 128), a_early, 0)
    collect(d_w_in, slice(512, 640), a_early, 64)
    weighted = d_w_out[...] * w_out[...].astype(F32)
    d_gain_out[...] = jnp.sum(weighted.T, axis=0, keepdims=True) / gain_out[...]
    settle(a_l, sems.at[23])
    collect(d_w_in, slice(0, 128), a_l, 0)
    collect(d_w_in, slice(128, 256), a_l, 64)
    settle(a_r, sems.at[27])
    collect(d_w_in, slice(256, 384), a_r, 0)
    collect(d_w_in, slice(384, 512), a_r, 64)
    weighted = d_w_in[...] * w_in[...].astype(F32)
    folded = weighted[:, 0:128]
    for b in range(1, 5):
        folded = folded + weighted[:, 128 * b : 128 * b + 128]
    d_gain_in[...] = jnp.sum(folded.T, axis=0, keepdims=True) / gain_in[...]

    store.wait()
    sent(s1l, 0)
    sent(s1r, 28)
    swap.wait_send()
    sent(r2a, 4)
    sent(r2b, 30)
    sent(s3a, 6)
    sent(s3b, 32)
    swap2.wait_send()
    sent(r4l, 12)
    sent(r4r, 14)
    finished(g_early, h_early, 1, 16)
    finished(g_l, h_l, 0, 20)
    finished(g_r, h_r, 1, 24)


def hand_over(*refs):
    sems = refs[10]
    stores = [
        pltpu.make_async_copy(src, dst, sems.at[n])
        for n, (src, dst) in enumerate(zip(refs[:5], refs[5:10]))
    ]
    for store in stores:
        store.start()
    for store in stores:
        store.wait()


def body(pair, pair_mask, proj_weight, out_weight, in_gain, out_gain, cotangent):
    vmem = pl.BlockSpec(memory_space=pltpu.VMEM)
    anywhere = pl.BlockSpec(memory_space=pl.ANY)
    V = pltpu.VMEM
    tiles = V((8, 128, 128), F32)
    tiles16 = V((8, 128, 128), BF16)
    by_tile = V((8, 1, 128), F32)
    lanes16 = V((128, 1024), BF16)
    sums = (V((128, 2, 128), BF16), V((256, 2, 128), BF16), V((2, 128), BF16), V((128, 2, 128), BF16))
    scratch = [
        V((128, 8, 128), BF16), V((128, 8, 128), BF16),
        V((8, 16, 8, 128), BF16), V((8, 16, 8, 128), BF16),
        V((8, 16, 4, 128), BF16), V((8, 16, 4, 128), BF16),
        V((128, 4, 128), BF16), V((128, 4, 128), BF16),
        V((128, 4, 128), BF16), V((128, 4, 128), BF16),
        V((8, 16, 4, 128), BF16), V((8, 16, 4, 128), BF16),
        V((8, 16, 8, 128), BF16), V((8, 16, 8, 128), BF16),
        V((128, 8, 128), BF16), V((128, 8, 128), BF16),
        V((512, 512), BF16), by_tile, V((640, 128), BF16), V((128, 128), BF16),
        V((128, 128), F32), V((128, 128), F32),
        tiles, by_tile, lanes16, tiles16, tiles16, tiles, tiles, tiles, tiles,
        lanes16, tiles, tiles, by_tile, V((256, 512), BF16), V((256, 512), BF16),
        V((256, 512), F32), V((256, 512), BF16), V((256, 512), BF16),
        tiles, lanes16, tiles16, V((8, 4, 8, 512), F32), V((2, 256, 512), BF16),
        tiles, tiles, V((640, 1024), BF16),
        *sums, *sums, *sums,
        V(pair.shape, BF16), V(pair_mask.shape, jnp.int32), V((128, 640), BF16), V((128, 128), BF16),
        V((1, 128), F32), V((1, 128), F32), V(pair.shape, BF16), V(pair.shape, F32),
        pltpu.SemaphoreType.DMA((8,)),
        pltpu.SemaphoreType.DMA((34,)),
    ]
    outs = pl.pallas_call(
        kernel,
        out_shape=(
            jax.ShapeDtypeStruct(pair.shape, F32),
            jax.ShapeDtypeStruct((128, 640), F32),
            jax.ShapeDtypeStruct((128, 128), F32),
            jax.ShapeDtypeStruct((1, 128), F32),
            jax.ShapeDtypeStruct((1, 128), F32),
        ),
        in_specs=[pl.BlockSpec(memory_space=pltpu.HBM)] * 7,
        out_specs=[anywhere] + [vmem] * 4,
        scratch_shapes=scratch,
        name="triangle_back",
        compiler_params=pltpu.CompilerParams(collective_id=0, has_side_effects=True, vmem_limit_bytes=24 * 2**20),
    )(
        *(
            pltpu.with_memory_space_constraint(x, pltpu.HBM)
            for x in (
                pair, pair_mask, proj_weight, out_weight,
                in_gain.reshape(1, 128), out_gain.reshape(1, 128), cotangent,
            )
        )
    )
    outs = pl.pallas_call(
        hand_over,
        out_shape=tuple(jax.ShapeDtypeStruct(x.shape, x.dtype) for x in outs),
        in_specs=[anywhere] * 5,
        out_specs=[pl.BlockSpec(memory_space=pltpu.HBM)] * 5,
        scratch_shapes=[pltpu.SemaphoreType.DMA((5,))],
        compiler_params=pltpu.CompilerParams(vmem_limit_bytes=2 * 2**20),
        name="hand_over",
    )(*outs)
    return (*outs[:3], outs[3].reshape(128), outs[4].reshape(128))


def solution(mesh):
    in_specs = (P("row", "col", None), P("row", "col"), P(), P(), P(), P(), P("row", "col", None))
    out_specs = (P("row", "col", None), P(), P(), P(), P())
    return jax.shard_map(body, mesh=mesh, in_specs=in_specs, out_specs=out_specs, check_vma=False)
```

```python
import jax
import jax.numpy as jnp
from jax import lax
from jax.experimental import pallas as pl
from jax.experimental.pallas import tpu as pltpu
from jax.sharding import PartitionSpec as P

MESH = pl.DeviceIdType.MESH
F32 = jnp.float32
BF16 = jnp.bfloat16
EPS = 1e-05


def settle(ref, sem):
    pltpu.make_async_copy(ref, ref, sem).wait()


def wrap(value, size):
    return jnp.where(value >= size, value - size, value)


def dot(a, b):
    return jnp.dot(a, b, preferred_element_type=F32)


def dot_nt(a, b):
    return lax.dot_general(a, b, (((1,), (1,)), ((), ())), preferred_element_type=F32)


def dot_tn(a, b):
    return lax.dot_general(a, b, (((0,), (0,)), ((), ())), preferred_element_type=F32)


def mean0(x):
    return jnp.sum(x, axis=0, keepdims=True) * (1.0 / x.shape[0])


def normalize(x):
    centred = x - mean0(x)
    inverse = lax.rsqrt(mean0(centred * centred) + EPS)
    return centred * inverse, inverse


def sigmoid(x):
    return 1.0 / (1.0 + jnp.exp(-x))


def start(src, dst, send_sem, recv_sem, row, col):
    pltpu.make_async_remote_copy(
        src, dst, send_sem, recv_sem, device_id=(row, col), device_id_type=MESH
    ).start()


def keep_or_start(mine, src, dst, send_sem, recv_sem, row, col):
    @pl.when(mine)
    def _():
        pltpu.make_async_copy(src, dst, recv_sem).start()

    @pl.when(jnp.logical_not(mine))
    def _():
        start(src, dst, send_sem, recv_sem, row, col)


def kernel(
    pair_h, mask_h, w_in_h, w_out_h, gain_in_h, gain_out_h, cot_h,
    d_pair_h, d_w_in, d_w_out, d_gain_in, d_gain_out,
    s1l, s1r, r1l, r1r, s2a, s2b, r2a, r2b, s3a, s3b, r3a, r3b, s4l, s4r, r4l, r4r,
    lane_swap, cell_mask, w_in_t, w_out_t, gi, go,
    zhat, s_z, zn, left, right, a_left, b_left, a_right, b_right,
    dproj, upper, h, h_mean, m_left, m_right, part, part_out, part_in,
    tri, onorm, dtri, dtri_f, dtri_all, grad_l, grad_r, dlin,
    g_early, h_early, o_early, a_early, g_l, h_l, o_l, a_l, g_r, h_r, o_r, a_r,
    pair, mask, w_in, w_out, gain_in, gain_out, cot, d_pair,
    local_sems, sems,
):
    row = lax.axis_index("row")
    col = lax.axis_index("col")
    me = row * 16 + col
    chip = row * 8 + col // 2
    core = lax.rem(col, 2)
    half = row // 8
    row8 = lax.rem(row, 8)
    cell = row8 * 16 + col
    seat = col // 2
    beside = (row, col + 1 - 2 * core)
    mine = half == core
    scale = 1.0 / 512.0
    loads = [
        pltpu.make_async_copy(src, dst, local_sems.at[n])
        for n, (src, dst) in enumerate(
            (
                (w_in_h, w_in), (w_out_h, w_out), (gain_in_h, gain_in), (gain_out_h, gain_out),
                (mask_h, mask), (pair_h, pair), (cot_h, cot),
            )
        )
    ]
    for load in loads:
        load.start()
    barrier = pltpu.get_barrier_semaphore()

    def hello(a, first=0):
        to_row = wrap(row + a, 16)
        for b in range(first, 16):
            pl.semaphore_signal(
                barrier, inc=1, device_id=(to_row, wrap(col + b, 16)), device_id_type=MESH
            )

    def hello_row(a, carry):
        hello(a)
        return carry

    lax.fori_loop(7, 16, hello_row, 0)
    lax.fori_loop(1, 7, hello_row, 0)
    hello(0, 1)

    def iota(shape, axis):
        return lax.broadcasted_iota(jnp.int32, shape, axis)

    r_i, c_i = iota((128, 128), 0), iota((128, 128), 1)
    to_block = jnp.where(c_i == (r_i & 7) * 16 + (r_i >> 3), 1.0, 0.0).astype(BF16)
    to_tiles = jnp.where(c_i == (r_i & 15) * 8 + (r_i >> 4), 1.0, 0.0).astype(BF16)

    for load in loads[:6]:
        load.wait()
    w_in_t[...] = w_in[...].astype(F32).T.astype(BF16)
    w_out_t[...] = w_out[...].astype(F32).T.astype(BF16)
    gi[...] = jnp.broadcast_to(gain_in[...], (128, 128)).T
    go[...] = jnp.broadcast_to(gain_out[...], (128, 128)).T
    spread = jnp.where(iota((32, 128), 0) == (iota((32, 128), 1) & 31), 1.0, 0.0).astype(BF16)
    wide = dot(mask[...].astype(F32).astype(BF16), spread)
    wide = jnp.where((iota((32, 128), 0) >> 3) == (iota((32, 128), 1) >> 5), wide, 0.0)
    wide = wide[0:8] + wide[8:16] + wide[16:24] + wide[24:32]
    for j in range(8):
        cell_mask[j] = wide[j : j + 1]

    def tile(j):
        return pl.ds(pl.multiple_of(j * 128, 128), 128)

    def cells_in(ref, j):
        rows = jnp.concatenate([ref[8 * k + j] for k in range(4)], axis=0)
        return rows.astype(F32).T

    def project(j, carry):
        normed, inverse = normalize(cells_in(pair, j))
        zhat[j] = normed
        s_z[j] = inverse
        z = (normed * gi[...]).astype(BF16)
        zn[:, tile(j)] = z
        keep = cell_mask[j]
        lin = dot(w_in_t[0:256], z)
        sig = sigmoid(lin[128:256])
        value = keep * sig
        product = value * lin[0:128]
        left[j] = product.astype(BF16)
        a_left[j] = value
        b_left[j] = product * (1.0 - sig)
        lin = dot(w_in_t[256:512], z)
        sig = sigmoid(lin[128:256])
        value = keep * sig
        product = value * lin[0:128]
        right[j] = product.astype(BF16)
        a_right[j] = value
        b_right[j] = product * (1.0 - sig)
        return carry

    lax.fori_loop(0, 8, project, 0, unroll=2)

    def to_blocks(src, g):
        return dot(to_block, src[:, 16 * g : 16 * g + 16, :].reshape(128, 128)).reshape(
            16, 8, 128
        ).astype(BF16)

    for g in range(8):
        s1l[16 * g : 16 * g + 16] = to_blocks(left, g)
        s1r[16 * g : 16 * g + 16] = to_blocks(right, g)

    pl.semaphore_wait(barrier, 255)

    def to_chips(src, dst, k):
        there = dst.at[row8, col]

        def ring(a, first=0):
            to_row = wrap(row + a, 16)
            for b in range(first, 8):
                to_seat = wrap(seat + b, 8)
                start(
                    src.at[to_row * 8 + to_seat], there, sems.at[k], sems.at[k + 1],
                    to_row, 2 * to_seat + half,
                )

        def step(a, carry):
            ring(a)
            return carry

        keep_or_start(mine, src.at[chip], there, sems.at[k], sems.at[k + 1], *beside)
        ring(0, 1)
        lax.fori_loop(1, 16, step, 0)

    def to_cells(src, dst, k):
        there = dst.at[chip]
        base = core * 8

        def ring(a, first=0):
            block = wrap(row8 + a, 8)
            for b in range(first, 16):
                to_col = wrap(col + b, 16)
                start(
                    src.at[block, to_col], there, sems.at[k], sems.at[k + 1],
                    base + block, to_col,
                )

        def step(a, carry):
            ring(a)
            return carry

        keep_or_start(
            mine, src.at[row8, col], there, sems.at[k], sems.at[k + 1], base + row8, col
        )
        ring(0, 1)
        lax.fori_loop(1, 8, step, 0)

    def sent(ref, k):
        settle(ref.at[pl.ds(0, 127)], sems.at[k])

        @pl.when(jnp.logical_not(mine))
        def _():
            settle(ref.at[0], sems.at[k])

    to_chips(s1l, r1l, 0)
    to_chips(s1r, r1r, 28)

    l_i, l_o = iota((512, 512), 0), iota((512, 512), 1)
    lane_swap[...] = jnp.where(
        l_o == ((l_i & 96) << 2) + ((l_i >> 7) << 5) + (l_i & 31), 1.0, 0.0
    ).astype(BF16)

    def gates(j, carry):
        z = zn[:, tile(j)]
        sig = sigmoid(dot(w_in_t[512:640], z))
        c_t = cells_in(cot, j)
        c_sig = c_t * sig
        d_p = c_sig.astype(BF16)
        dproj[:, tile(j)] = d_p
        upper[j] = c_sig * (1.0 - sig)
        grad = dot(w_out[...], d_p) * go[...]
        h[j] = grad
        h_mean[j] = mean0(grad)
        return carry

    loads[6].wait()
    lax.fori_loop(0, 8, gates, 0, unroll=2)

    def flat(x):
        return x.astype(F32).reshape(64, 128).astype(BF16)

    def swapped(piece):
        x = jnp.concatenate(
            [
                jnp.concatenate([piece(quad, k) for k in range(4)], axis=1)
                for quad in range(4)
            ],
            axis=0,
        )
        return dot(x, lane_swap[...])

    def part_of(y, quad, k):
        return y[64 * quad : 64 * quad + 64, 128 * k : 128 * k + 128]

    for side, (landed, matrix) in enumerate(((r1l, m_left), (r1r, m_right))):
        settle(landed, sems.at[1 + 28 * side])
        y = swapped(lambda quad, k: flat(landed[:, 4 * quad + k])).astype(BF16)
        for quad in range(4):
            for k in range(4):
                matrix[64 * k : 64 * k + 64, 128 * quad : 128 * quad + 128] = part_of(y, quad, k)

    def columns(which):
        return m_left[:, pl.ds(pl.multiple_of(which * 256, 256), 256)]

    part_out[...] = dot_tn(columns(1 - core), m_right[...]).astype(BF16)
    swap = pltpu.make_async_remote_copy(
        part_out, part_in, sems.at[2], sems.at[3], device_id=beside, device_id_type=MESH
    )
    swap.start()
    part[...] = dot_tn(columns(core), m_right[...])
    swap.wait_recv()
    part[...] = part[...] + part_in[...].astype(F32)
    product = part.reshape(8, 4, 8, 512)

    def lanes(quad):
        return slice(128 * quad, 128 * quad + 128)

    y = swapped(lambda quad, k: product[:, k, :, lanes(quad)].reshape(64, 128).astype(BF16))
    for quad in range(4):
        for k in range(4):
            block = part_of(y, quad, k).reshape(8, 8, 128)
            s2a[:, 4 * quad + k] = block[:, 0:4].astype(BF16)
            s2b[:, 4 * quad + k] = block[:, 4:8].astype(BF16)

    to_cells(s2a, r2a, 4)
    to_cells(s2b, r2b, 30)

    def to_tile_rows(src, dst):
        for g in range(8):
            x = src(g).astype(F32).reshape(128, 128).astype(BF16)
            y = dot(to_tiles, x)
            for j in range(8):
                dst[j, 16 * g : 16 * g + 16, :] = y[16 * j : 16 * j + 16]


    def middle(j, carry):
        that, inverse = normalize(tri[j])
        o = (that * go[...]).astype(BF16)
        onorm[:, tile(j)] = o
        dlin[512:640, tile(j)] = (upper[j] * dot(w_out_t[...], o)).astype(BF16)
        grad = h[j]
        d_t = inverse * (grad - h_mean[j] - that * mean0(grad * that))
        dtri[j] = d_t.astype(BF16)
        return carry

    to_half_block = jnp.where(c_i == (r_i & 3) * 32 + (r_i >> 2), 1.0, 0.0).astype(BF16)
    to_half_tiles = jnp.where(c_i == (r_i & 31) * 4 + (r_i >> 5), 1.0, 0.0).astype(BF16)

    def middle_half(landed, leaving, landed_sem, first):
        settle(landed, sems.at[landed_sem])
        for g in range(4):
            channels = slice(32 * g, 32 * g + 32)
            y = dot(to_half_tiles, landed[channels].astype(F32).reshape(128, 128).astype(BF16))
            for j in range(4):
                tri[first + j, channels, :] = y[32 * j : 32 * j + 32]
        lax.fori_loop(first, first + 4, middle, 0, unroll=2)
        for g in range(4):
            channels = slice(32 * g, 32 * g + 32)
            y = dot(to_half_block, dtri[first : first + 4, channels, :].reshape(128, 128))
            leaving[channels] = y.reshape(32, 4, 128).astype(BF16)

    middle_half(r2a, s3a, 5, 0)
    to_chips(s3a, r3a, 6)
    middle_half(r2b, s3b, 31, 4)
    to_chips(s3b, r3b, 32)

    def fill(dst, value):
        rows = value.astype(BF16)
        for b in range(2):
            for i in range(64):
                dst[64 * b + i] = rows[2 * i : 2 * i + 2, 128 * b : 128 * b + 128]

    def owner(to_seat, flip):
        return lax.rem(to_seat + flip, 2)

    def scatter(src, dst, flip, k):
        there = dst.at[me]

        def ring(a, first=0):
            to_row = wrap(row + a, 16)
            for b in range(first, 8):
                to_seat = wrap(seat + b, 8)
                start(
                    src.at[to_row * 8 + to_seat], there, sems.at[k], sems.at[k + 1],
                    to_row, 2 * to_seat + owner(to_seat, flip),
                )

        def step(a, carry):
            ring(a)
            return carry

        keep_or_start(
            owner(seat, flip) == core, src.at[chip], there, sems.at[k], sems.at[k + 1], *beside
        )
        lax.fori_loop(6, 16, step, 0)
        lax.fori_loop(1, 6, step, 0)
        ring(0, 1)

    def gather(held, total, dst, flip, k):
        @pl.when(owner(seat, flip) == core)
        def _():
            settle(held, sems.at[k + 1])
            total[...] = jnp.sum(held[...].astype(F32), axis=0).astype(BF16)
            there = dst.at[chip]

            def ring(a, first=0):
                to_row = wrap(row + a, 16)
                for b in range(first, 16):
                    start(
                        total, there, sems.at[k + 2], sems.at[k + 3],
                        to_row, wrap(col + b, 16),
                    )

            def step(a, carry):
                ring(a)
                return carry

            pltpu.make_async_copy(total, there, sems.at[k + 3]).start()
            lax.fori_loop(6, 16, step, 0)
            lax.fori_loop(1, 6, step, 0)
            ring(0, 1)

    def finished(src, held, flip, k):
        settle(src.at[pl.ds(0, 127)], sems.at[k])

        @pl.when(owner(seat, flip) != core)
        def _():
            settle(src.at[0], sems.at[k])

        @pl.when(owner(seat, flip) == core)
        def _():
            settle(held.at[pl.ds(0, 255)], sems.at[k + 2])

    fill(
        g_early,
        jnp.concatenate(
            [dot_nt(onorm[...], dproj[...]), dot_nt(zn[...], dlin[512:640])], axis=1
        ),
    )

    settle(r3a, sems.at[7])
    settle(r3b, sems.at[33])

    def joined(q):
        both = jnp.concatenate([r3a[:, q].astype(F32), r3b[:, q].astype(F32)], axis=1)
        return both.reshape(64, 128).astype(BF16)

    y = swapped(lambda quad, k: joined(4 * quad + k))
    for quad in range(4):
        for k in range(4):
            dtri_f[:, k, :, lanes(quad)] = part_of(y, quad, k).reshape(8, 8, 128)
    d_own = dtri_f[...].reshape(256, 512).astype(BF16)
    dtri_all[core] = d_own
    swap2 = pltpu.make_async_remote_copy(
        dtri_all.at[core], dtri_all.at[core], sems.at[10], sems.at[11],
        device_id=beside, device_id_type=MESH,
    )
    swap2.start()

    def leave_half(grad, dst, which):
        x = jnp.concatenate(
            [
                jnp.concatenate(
                    [grad[64 * k : 64 * k + 64, lanes(quad)] for k in range(4)], axis=1
                )
                for quad in range(2)
            ],
            axis=0,
        )
        y = dot(x, lane_swap[...])
        for quad in range(2):
            for k in range(4):
                dst[:, 8 * which + 4 * quad + k] = (
                    part_of(y, quad, k).reshape(8, 8, 128).astype(BF16)
                )

    def half_to_cells(src, dst, which, k):
        there = dst.at[chip]
        base = core * 8
        spot = lax.rem(col, 8)

        def ring(a, first=0):
            block = wrap(row8 + a, 8)
            for b in range(first, 8):
                to_col = 8 * which + wrap(spot + b, 8)
                start(
                    src.at[block, to_col], there, sems.at[k], sems.at[k + 1],
                    base + block, to_col,
                )

        def step(a, carry):
            ring(a)
            return carry

        to_col = 8 * which + spot
        keep_or_start(
            jnp.logical_and(mine, to_col == col), src.at[row8, to_col], there,
            sems.at[k], sems.at[k + 1], base + row8, to_col,
        )
        ring(0, 1)
        lax.fori_loop(1, 8, step, 0)

    leave_half(dot_nt(m_right[...], d_own).astype(BF16), s4l, core)
    half_to_cells(s4l, r4l, core, 12)
    swap2.wait_recv()
    leave_half(dot_nt(m_right[...], dtri_all[1 - core]).astype(BF16), s4l, 1 - core)
    half_to_cells(s4l, r4l, 1 - core, 12)
    d_all = dtri_all[...].reshape(512, 512)

    def leave(grad, dst):
        y = swapped(lambda quad, k: grad[64 * k : 64 * k + 64, lanes(quad)])
        for quad in range(4):
            for k in range(4):
                dst[:, 4 * quad + k] = part_of(y, quad, k).reshape(8, 8, 128).astype(BF16)

    leave(dot(m_left[...], d_all).astype(BF16), s4r)
    to_cells(s4r, r4r, 14)

    def back(grad, value, slope, base):
        def step(j, carry):
            d = grad[j]
            dlin[base : base + 128, tile(j)] = (d * value[j]).astype(BF16)
            dlin[base + 128 : base + 256, tile(j)] = (d * slope[j]).astype(BF16)
            return carry

        lax.fori_loop(0, 8, step, 0, unroll=2)

    settle(r4l, sems.at[13])
    to_tile_rows(lambda g: r4l[16 * g : 16 * g + 16], grad_l)
    back(grad_l, a_left, b_left, 0)
    fill(g_l, dot_nt(zn[...], dlin[0:256]))
    scatter(g_l, h_l, 0, 20)
    scatter(g_early, h_early, 1, 16)

    settle(r4r, sems.at[15])
    to_tile_rows(lambda g: r4r[16 * g : 16 * g + 16], grad_r)
    back(grad_r, a_right, b_right, 256)
    fill(g_r, dot_nt(zn[...], dlin[256:512]))
    scatter(g_r, h_r, 1, 24)

    gather(h_early, o_early, a_early, 1, 16)
    gather(h_l, o_l, a_l, 0, 20)

    def finish(j, carry):
        g = dot(w_in[...], dlin[:, tile(j)]) * gi[...]
        normed = zhat[j]
        d = s_z[j] * (g - mean0(g) - normed * mean0(g * normed))
        d = d.T
        for k in range(4):
            d_pair[8 * k + j] = d[32 * k : 32 * k + 32]
        return carry

    lax.fori_loop(0, 4, finish, 0, unroll=2)
    gather(h_r, o_r, a_r, 1, 24)
    lax.fori_loop(4, 8, finish, 0, unroll=2)
    store = pltpu.make_async_copy(d_pair, d_pair_h, local_sems.at[7])
    store.start()

    def collect(dst, lanes, src, base):
        for i in range(64):
            dst[2 * i : 2 * i + 2, lanes] = src[base + i].astype(F32) * scale

    settle(a_early, sems.at[19])
    collect(d_w_out, slice(0, 128), a_early, 0)
    collect(d_w_in, slice(512, 640), a_early, 64)
    weighted = d_w_out[...] * w_out[...].astype(F32)
    d_gain_out[...] = jnp.sum(weighted.T, axis=0, keepdims=True) / gain_out[...]
    settle(a_l, sems.at[23])
    collect(d_w_in, slice(0, 128), a_l, 0)
    collect(d_w_in, slice(128, 256), a_l, 64)
    settle(a_r, sems.at[27])
    collect(d_w_in, slice(256, 384), a_r, 0)
    collect(d_w_in, slice(384, 512), a_r, 64)
    weighted = d_w_in[...] * w_in[...].astype(F32)
    folded = weighted[:, 0:128]
    for b in range(1, 5):
        folded = folded + weighted[:, 128 * b : 128 * b + 128]
    d_gain_in[...] = jnp.sum(folded.T, axis=0, keepdims=True) / gain_in[...]

    store.wait()
    sent(s1l, 0)
    sent(s1r, 28)
    swap.wait_send()
    sent(r2a, 4)
    sent(r2b, 30)
    sent(s3a, 6)
    sent(s3b, 32)
    swap2.wait_send()
    sent(r4l, 12)
    sent(r4r, 14)
    finished(g_early, h_early, 1, 16)
    finished(g_l, h_l, 0, 20)
    finished(g_r, h_r, 1, 24)


def hand_over(*refs):
    sems = refs[10]
    stores = [
        pltpu.make_async_copy(src, dst, sems.at[n])
        for n, (src, dst) in enumerate(zip(refs[:5], refs[5:10]))
    ]
    for store in stores:
        store.start()
    for store in stores:
        store.wait()


def body(pair, pair_mask, proj_weight, out_weight, in_gain, out_gain, cotangent):
    vmem = pl.BlockSpec(memory_space=pltpu.VMEM)
    anywhere = pl.BlockSpec(memory_space=pl.ANY)
    V = pltpu.VMEM
    tiles = V((8, 128, 128), F32)
    tiles16 = V((8, 128, 128), BF16)
    by_tile = V((8, 1, 128), F32)
    lanes16 = V((128, 1024), BF16)
    sums = (V((128, 2, 128), BF16), V((256, 2, 128), BF16), V((2, 128), BF16), V((128, 2, 128), BF16))
    scratch = [
        V((128, 8, 128), BF16), V((128, 8, 128), BF16),
        V((8, 16, 8, 128), BF16), V((8, 16, 8, 128), BF16),
        V((8, 16, 4, 128), BF16), V((8, 16, 4, 128), BF16),
        V((128, 4, 128), BF16), V((128, 4, 128), BF16),
        V((128, 4, 128), BF16), V((128, 4, 128), BF16),
        V((8, 16, 4, 128), BF16), V((8, 16, 4, 128), BF16),
        V((8, 16, 8, 128), BF16), V((8, 16, 8, 128), BF16),
        V((128, 8, 128), BF16), V((128, 8, 128), BF16),
        V((512, 512), BF16), by_tile, V((640, 128), BF16), V((128, 128), BF16),
        V((128, 128), F32), V((128, 128), F32),
        tiles, by_tile, lanes16, tiles16, tiles16, tiles, tiles, tiles, tiles,
        lanes16, tiles, tiles, by_tile, V((256, 512), BF16), V((256, 512), BF16),
        V((256, 512), F32), V((256, 512), BF16), V((256, 512), BF16),
        tiles, lanes16, tiles16, V((8, 4, 8, 512), F32), V((2, 256, 512), BF16),
        tiles, tiles, V((640, 1024), BF16),
        *sums, *sums, *sums,
        V(pair.shape, BF16), V(pair_mask.shape, jnp.int32), V((128, 640), BF16), V((128, 128), BF16),
        V((1, 128), F32), V((1, 128), F32), V(pair.shape, BF16), V(pair.shape, F32),
        pltpu.SemaphoreType.DMA((8,)),
        pltpu.SemaphoreType.DMA((34,)),
    ]
    outs = pl.pallas_call(
        kernel,
        out_shape=(
            jax.ShapeDtypeStruct(pair.shape, F32),
            jax.ShapeDtypeStruct((128, 640), F32),
            jax.ShapeDtypeStruct((128, 128), F32),
            jax.ShapeDtypeStruct((1, 128), F32),
            jax.ShapeDtypeStruct((1, 128), F32),
        ),
        in_specs=[pl.BlockSpec(memory_space=pltpu.HBM)] * 7,
        out_specs=[anywhere] + [vmem] * 4,
        scratch_shapes=scratch,
        name="triangle_back",
        compiler_params=pltpu.CompilerParams(collective_id=0, has_side_effects=True, vmem_limit_bytes=24 * 2**20),
    )(
        *(
            pltpu.with_memory_space_constraint(x, pltpu.HBM)
            for x in (
                pair, pair_mask, proj_weight, out_weight,
                in_gain.reshape(1, 128), out_gain.reshape(1, 128), cotangent,
            )
        )
    )
    outs = pl.pallas_call(
        hand_over,
        out_shape=tuple(jax.ShapeDtypeStruct(x.shape, x.dtype) for x in outs),
        in_specs=[anywhere] * 5,
        out_specs=[pl.BlockSpec(memory_space=pltpu.HBM)] * 5,
        scratch_shapes=[pltpu.SemaphoreType.DMA((5,))],
        compiler_params=pltpu.CompilerParams(vmem_limit_bytes=2 * 2**20),
        name="hand_over",
    )(*outs)
    return (*outs[:3], outs[3].reshape(128), outs[4].reshape(128))


def solution(mesh):
    in_specs = (P("row", "col", None), P("row", "col"), P(), P(), P(), P(), P("row", "col", None))
    out_specs = (P("row", "col", None), P(), P(), P(), P())
    return jax.shard_map(body, mesh=mesh, in_specs=in_specs, out_specs=out_specs, check_vma=False)
```
